32 devices in a mesh: fsdp: 32 (over z, y, x, core).
Axes of the slice: x: 2, y: 2, z: 4, core: 2. Of those that a mesh axis runs over, the one named last changes fastest.
Arguments:
- tokens: bfloat16 [4096, 2048], P('fsdp'), may hold values from -6 to 6
- cotangent: bfloat16 [4096, 2048], P('fsdp'), may hold values from -6 to 6
- segment_ids: int32 [4096], P('fsdp'), may hold values from 0 to 7, never falling along the last dimension, each value on 1 to 1024 neighbouring positions
- expert_ids: int32 [4096, 4], P('fsdp'), may hold values from 0 to 7, all different within a row
- route_weights: float32 [4096, 4], P('fsdp'), may hold values from 0.2 to 0.6
- pair_order: int32 [32, 512], P('fsdp'), may hold values from 0 to 511, each once within a row
- norm_in_gain: bfloat16 [2048], P('fsdp'), may hold values from 0.5 to 1.5
- qkv_weight: bfloat16 [2048, 6144], P('fsdp'), may hold values from -0.125 to 0.125
- qkv_bias: bfloat16 [6144], P('fsdp'), may hold values from -1.5 to 1.5
- out_weight: bfloat16 [2048, 2048], P('fsdp'), may hold values from -0.5 to 0.5
- norm_mid_gain: bfloat16 [2048], P('fsdp'), may hold values from 0.5 to 1.5
- shared_gate: bfloat16 [2048], P('fsdp'), may hold values from -0.125 to 0.125
- shared_in: bfloat16 [2048, 11264], P('fsdp'), may hold values from -0.125 to 0.125
- shared_out: bfloat16 [5632, 2048], P('fsdp'), may hold values from -0.078125 to 0.078125
- expert_in: bfloat16 [32, 2048, 704], P('fsdp'), may hold values from -0.125 to 0.125
- expert_out: bfloat16 [32, 352, 2048], P('fsdp'), may hold values from -0.15625 to 0.15625
Outputs:
- output: bfloat16 [4096, 2048], P('fsdp')
- input_grad: float32 [4096, 2048], P('fsdp')
- norm_in_gain_grad: float32 [2048], P('fsdp')
- qkv_weight_grad: float32 [2048, 6144], P('fsdp')
- qkv_bias_grad: float32 [6144], P('fsdp')
- out_weight_grad: float32 [2048, 2048], P('fsdp')
- norm_mid_gain_grad: float32 [2048], P('fsdp')
- shared_gate_grad: float32 [2048], P('fsdp')
- shared_in_grad: float32 [2048, 11264], P('fsdp')
- shared_out_grad: float32 [5632, 2048], P('fsdp')
- expert_in_grad: float32 [32, 2048, 704], P('fsdp')
- expert_out_grad: float32 [32, 352, 2048], P('fsdp')
The draws below stay inside these ranges and needn't reach their ends.
Inputs may be any that keep to these rules, and one draw needn't show every extreme that they name: `segment_ids`: ids never fall along the tokens; each sequence holds 1 to 1024 tokens and one holds exactly 1024. `expert_ids`: each token names 4 different experts. `pair_order`: each row is a permutation of that device's pairs; pair t * 4 + k is local token t's k-th expert.
All inputs are finite; a program needn't handle non-finite values.
Results may differ from the reference program's by a relative error of at most 0.015.
Values may be sent and summed in bfloat16 or wider, within the bound.
A program may use at most 576 MiB of HBM per device.

```python
import math
import jax
import jax.numpy as jnp
import numpy as np
from jax import lax

D = 2048
HEADS = 16
HEAD_DIM = 128
FE = 1408
FS = 5632
TOP = 4
EXP_PARTS = 4
SEQ = 1024
TOK_DEV = 128
SHARDS = 32
TOKENS = 4096
EXPERTS = 8
CAP = 72
SPAN = 8
SEGS = 8
N_FSDP = 32


def block_levels(key, shape, cuts, least, largest):
    def one(dim, blocks):
        steps = jax.random.uniform(jax.random.fold_in(jax.random.fold_in(key, 6), dim), (blocks,), jnp.float32, least / len(cuts), largest / len(cuts))
        return jnp.repeat(jnp.exp(steps), shape[dim] // blocks).reshape((-1,) + (1,) * (len(shape) - dim - 1))

    gain = one(*cuts[0])
    for cut in cuts[1:]:
        gain = gain * one(*cut)
    return gain


def choose_distinct(rng, rows, count, top, lift):
    sequence = jax.random.permutation(jax.random.fold_in(rng, 1), count)
    pull = sequence
    for power in range(3):
        pull = pull * pull // count
    pull = pull * lift // count
    lots = jax.random.randint(jax.random.fold_in(rng, 2), (rows, count), 0, 4096) + pull
    fixed_rows = jax.random.permutation(jax.random.fold_in(rng, 3), rows)[jnp.arange(count) % rows]
    lots = jnp.where(jnp.arange(rows)[:, None] == fixed_rows[None, :], 1 << 14, lots)
    priority = lots * count + jnp.arange(count)
    return lax.top_k(priority.astype(jnp.int32), top)[1].astype(jnp.int32)


def split_up(number_of, total, most, slope):
    weights = [(1 << 20) // math.isqrt(grade ** slope) + 1 for grade in range(2, number_of + 1)]
    spare, counts = total - most - (number_of - 1), [1] * (number_of - 1)
    while spare > 0:
        free = [i for i in range(number_of - 1) if counts[i] < most]
        pool, budget = sum([weights[i] for i in free]), spare
        for i in free:
            addition = min(most - counts[i], max(1, budget * weights[i] // pool), spare)
            counts[i] = counts[i] + addition
            spare = spare - addition
    return np.array([most] + counts)


def uneven_parts(stream_key, number_of, total, bound, lean):
    if number_of == 2:
        one = jax.random.randint(stream_key, (), max(1, total - bound), min(bound, total - 1) + 1)
        return jnp.stack([one, total - one])
    tallies = jnp.asarray(split_up(number_of, total, bound, lean), jnp.int32)
    couples = (number_of - 1) // 2
    source_of, receiver = tallies[1:1 + 2 * couples:2], tallies[2:2 + 2 * couples:2]
    margin = jnp.minimum(source_of - 1, bound - receiver)
    passed = jax.random.randint(jax.random.fold_in(stream_key, 1), (couples,), 0, 1 << 20) % (margin + 1)
    tallies = tallies.at[1:1 + 2 * couples:2].set(source_of - passed).at[2:2 + 2 * couples:2].set(receiver + passed)
    return tallies[jax.random.permutation(jax.random.fold_in(stream_key, 2), number_of)]


def noise(stream_key, extent, spread, bound, cuts=(), held_as=jnp.bfloat16):
    drawn = spread * jax.random.normal(stream_key, extent, jnp.float32)
    if cuts:
        drawn = drawn * block_levels(stream_key, extent, cuts, -0.22, 0.18)
    return jnp.clip(drawn, -bound, bound).astype(held_as)


def setup_inputs(seed: int = 0) -> dict:
    key_list = jax.random.split(jax.random.key(seed), 17)
    return {
        "tokens": noise(key_list[0], (TOKENS, D), 1.0, 6.0, ((0, 32),)),
        "cotangent": noise(key_list[1], (TOKENS, D), 1.0, 6.0, ((0, 32),)),
        "segment_ids": jnp.searchsorted(jnp.cumsum(uneven_parts(key_list[2], SEGS, TOKENS, SEQ, 1)), jnp.arange(TOKENS), side="right").astype(jnp.int32),
        "expert_ids": choose_distinct(key_list[3], TOKENS, EXPERTS, TOP, 4096),
        "route_weights": jnp.clip(0.2 + 0.400000021 * jax.random.uniform(key_list[4], (TOKENS, TOP), jnp.float32) ** block_levels(key_list[4], (TOKENS, TOP), ((0, 32),), -0.2, 0.2), 0.2, 0.6),
        "pair_order": jax.vmap(lambda own: jax.random.permutation(own, TOK_DEV * TOP))(jax.random.split(key_list[5], SHARDS)).reshape((SHARDS, TOK_DEV * TOP)).astype(jnp.int32),
        "norm_in_gain": jnp.clip(1.0 + 0.1 * jax.random.normal(key_list[6], (D,), jnp.float32), 0.5, 1.5).astype(jnp.bfloat16),
        "qkv_weight": noise(key_list[7], (D, 3 * D), D ** -0.5, 0.125, ((0, 32),)),
        "qkv_bias": noise(key_list[8], (3 * D,), 0.3, 1.5, ((0, 32),)),
        "out_weight": noise(key_list[9], (D, D), (D // 16) ** -0.5, 0.5, ((0, 32),)),
        "norm_mid_gain": jnp.clip(1.0 + 0.1 * jax.random.normal(key_list[10], (D,), jnp.float32), 0.5, 1.5).astype(jnp.bfloat16),
        "shared_gate": noise(key_list[11], (D,), D ** -0.5, 0.125, ((0, 32),)),
        "shared_in": noise(key_list[12], (D, 2 * FS), D ** -0.5, 0.125, ((0, 32),)),
        "shared_out": noise(key_list[13], (FS, D), FS ** -0.5, 0.078125, ((0, 32),)),
        "expert_in": noise(key_list[14], (EXPERTS * EXP_PARTS, D, 2 * FE // EXP_PARTS), D ** -0.5, 0.125, ((0, 32),)),
        "expert_out": noise(key_list[15], (EXPERTS * EXP_PARTS, FE // EXP_PARTS, D), FE ** -0.5, 0.15625, ((0, 32),)),
    }


@jax.custom_vjp
def low(v):
    return lax.optimization_barrier(v.astype(jnp.bfloat16)).astype(jnp.float32)

@jax.custom_vjp
def low_back(v):
    return v

def low_keep(v):
    return (low(v), None)

def low_pass(kept, grad):
    return (grad,)

def back_keep(v):
    return (v, None)

def back_low(kept, grad):
    return (low(grad),)
low.defvjp(low_keep, low_pass)
low_back.defvjp(back_keep, back_low)
EPSILON = 1e-06
THETA = 1000000.0
MASKED = -1e+30
HIGHEST = lax.Precision.HIGHEST

def rms_norm(vector, factor):
    return vector * lax.rsqrt(lax.optimization_barrier(jnp.mean(vector * vector, axis=-1, keepdims=True)) + EPSILON) * factor

def rotate(vector, cosine, sine_table):
    middle = vector.shape[-1] // 2
    turned = jnp.concatenate([-vector[..., middle:], vector[..., :middle]], axis=-1)
    return vector * cosine + turned * sine_table

def swiglu(joined):
    middle = joined.shape[-1] // 2
    return jax.nn.silu(joined[..., :middle]) * joined[..., middle:]

def matmul(left, right):
    return jnp.dot(left, right, precision=HIGHEST, preferred_element_type=jnp.float32)

def reference(tokens, cotangent, segment_ids, expert_ids, route_weights, pair_order, norm_in_gain, qkv_weight, qkv_bias, out_weight, norm_mid_gain, shared_gate, shared_in, shared_out, expert_in, expert_out):
    part_width = FE // EXP_PARTS
    window = (SPAN + 1) * TOK_DEV
    lead = SPAN * TOK_DEV
    score_scale = HEAD_DIM ** (-0.5)
    seg_counts = jax.ops.segment_sum(jnp.ones((TOKENS,), jnp.int32), segment_ids, num_segments=SEGS)
    seg_starts = (jnp.cumsum(seg_counts, dtype=jnp.int32) - seg_counts).astype(jnp.int32)
    positions = (jnp.arange(TOKENS, dtype=jnp.int32) - seg_starts[segment_ids]).astype(jnp.float32)
    inverse = THETA ** (-jnp.arange(0, HEAD_DIM, 2, dtype=jnp.float32) / HEAD_DIM)
    angles = positions[:, None] * inverse[None, :]
    angles = jnp.concatenate([angles, angles], axis=-1)[:, None, :]
    cosine = jnp.cos(angles)
    sine_table = jnp.sin(angles)
    flat_experts = expert_ids.reshape(N_FSDP, TOK_DEV * TOP)
    ranked = jnp.take_along_axis(flat_experts, pair_order, axis=1)
    onehot = (ranked[:, :, None] == jnp.arange(EXPERTS, dtype=jnp.int32)[None, None, :]).astype(jnp.int32)
    running = jnp.cumsum(onehot, axis=1, dtype=jnp.int32)
    slot_ranked = (lax.optimization_barrier(jnp.sum(running * onehot, axis=-1, dtype=jnp.int32)) - 1).astype(jnp.int32)
    device_rows = jnp.broadcast_to(jnp.arange(N_FSDP, dtype=jnp.int32)[:, None], pair_order.shape)
    slots = jnp.zeros_like(flat_experts).at[device_rows, pair_order].set(slot_ranked)
    kept_pairs = slots < CAP
    slot_place = (flat_experts * (N_FSDP * CAP) + device_rows * CAP + slots).astype(jnp.int32)
    slot_place = jnp.where(kept_pairs, slot_place, EXPERTS * N_FSDP * CAP).reshape(-1)
    slot_pick = jnp.where(kept_pairs.reshape(-1), slot_place, 0)
    kept_float = kept_pairs.reshape(-1).astype(jnp.float32)
    pair_weights = route_weights.astype(jnp.float32).reshape(-1)
    key_ids_pad = jnp.concatenate([jnp.full((lead,), -1, jnp.int32), segment_ids])
    causal = jnp.arange(window, dtype=jnp.int32)[None, :] <= jnp.arange(TOK_DEV, dtype=jnp.int32)[:, None] + lead

    def forward(inputs, gain_in, weight_qkv, bias_qkv, weight_out, gain_mid, gate_vector, weight_shared_in, weight_shared_out, weight_expert_in, weight_expert_out):
        normed = low(rms_norm(inputs, gain_in))
        projected = low_back(matmul(normed, weight_qkv) + bias_qkv)
        queries = low(rotate(projected[:, :D].reshape(TOKENS, HEADS, HEAD_DIM), cosine, sine_table))
        key_rows = low(rotate(projected[:, D:2 * D].reshape(TOKENS, HEADS, HEAD_DIM), cosine, sine_table))
        values = low(projected[:, 2 * D:].reshape(TOKENS, HEADS, HEAD_DIM))
        key_pad = jnp.concatenate([jnp.zeros((lead, HEADS, HEAD_DIM), jnp.float32), key_rows])
        value_pad = jnp.concatenate([jnp.zeros((lead, HEADS, HEAD_DIM), jnp.float32), values])

        def block(block_index):
            first_row = (block_index * TOK_DEV).astype(jnp.int32)
            query_block = lax.dynamic_slice_in_dim(queries, first_row, TOK_DEV, 0)
            key_block = lax.dynamic_slice_in_dim(key_pad, first_row, window, 0)
            value_block = lax.dynamic_slice_in_dim(value_pad, first_row, window, 0)
            query_ids = lax.dynamic_slice_in_dim(segment_ids, first_row, TOK_DEV, 0)
            key_ids = lax.dynamic_slice_in_dim(key_ids_pad, first_row, window, 0)
            allowed = causal & (key_ids[None, :] == query_ids[:, None])
            scores = low_back(jnp.einsum('qhd,khd->hqk', query_block, key_block, precision=HIGHEST) * score_scale)
            scores = jnp.where(allowed[None], scores, MASKED)
            probs = low(jax.nn.softmax(scores, axis=-1))
            return jnp.einsum('hqk,khd->qhd', probs, value_block, precision=HIGHEST)
        attended = lax.map(jax.checkpoint(block), jnp.arange(N_FSDP, dtype=jnp.int32))
        attended = low_back(low(attended.reshape(TOKENS, D)))
        hidden = inputs + low_back(matmul(attended, weight_out))
        mid = low(rms_norm(hidden, gain_mid))
        shared_pre = low_back(matmul(mid, weight_shared_in))
        shared_act = low(swiglu(shared_pre))
        shared_value = low_back(matmul(shared_act, weight_shared_out))
        shared_scale = jax.nn.sigmoid(matmul(mid, gate_vector))
        pair_rows = jnp.repeat(mid, TOP, axis=0)
        slot_table = jnp.zeros((EXPERTS * N_FSDP * CAP, D), jnp.float32).at[slot_place].set(pair_rows, mode='drop')

        def expert_block(pieces):
            rows_in, weight_in, weight_down = pieces
            pre = low_back(jnp.einsum('rd,qdf->qrf', rows_in, weight_in, precision=HIGHEST))
            act = low(swiglu(pre))
            partial_value = low_back(low(jnp.einsum('qrf,qfd->qrd', act, weight_down, precision=HIGHEST)))
            return lax.optimization_barrier(jnp.sum(partial_value, axis=0))
        results = lax.map(jax.checkpoint(expert_block), (slot_table.reshape(EXPERTS, N_FSDP * CAP, D), weight_expert_in.reshape(EXPERTS, EXP_PARTS, D, 2 * part_width), weight_expert_out.reshape(EXPERTS, EXP_PARTS, part_width, D)))
        pair_out = results.reshape(-1, D)[slot_pick] * kept_float[:, None]
        routed = lax.optimization_barrier(jnp.sum((pair_out * pair_weights[:, None]).reshape(TOKENS, TOP, D), axis=1))
        return hidden + routed + shared_scale[:, None] * shared_value
    primals = (tokens.astype(jnp.float32), norm_in_gain.astype(jnp.float32), qkv_weight.astype(jnp.float32), qkv_bias.astype(jnp.float32), out_weight.astype(jnp.float32), norm_mid_gain.astype(jnp.float32), shared_gate.astype(jnp.float32), shared_in.astype(jnp.float32), shared_out.astype(jnp.float32), expert_in.astype(jnp.float32), expert_out.astype(jnp.float32))
    result, pullback = jax.vjp(forward, *primals)
    grads = pullback(cotangent.astype(jnp.float32))
    return (result.astype(jnp.bfloat16), grads[0], grads[1], grads[2], grads[3], grads[4], grads[5], grads[6], grads[7], grads[8], grads[9], grads[10])
```

```python
import functools

import jax
import jax.numpy as jnp
from jax import lax
from jax.experimental import pallas as pl
from jax.experimental.pallas import tpu as pltpu
from jax.sharding import PartitionSpec as P

HEAD_DIM = 128
EXP_PARTS = 4
SEQ = 1024

EPSILON = 1e-06
THETA = 1000000.0
MASKED = -1e30
BF = jnp.bfloat16
FL = jnp.float32
AXIS = "fsdp"
MESH = pl.DeviceIdType.MESH
PLAN = {
    1: (("f", 0), ("s", 0), ("z", 0)),
    4: (("f", 0), ("f", 1), ("s", 0), ("f", 2), ("s", 1), ("f", 3), ("z", 0), ("s", 2), ("z", 1),
        ("s", 3), ("z", 2), ("z", 3)),
}


def place(length):
    me = lax.axis_index(AXIS)
    z, y, x, c = me // 8, (me // 4) % 2, (me // 2) % 2, me % 2

    def device(dz=0, y=y, x=x, c=c):
        return (((z + dz) * 2 + y) * 2 + x) * 2 + c

    return (z if length > 1 else z * 0), y, x, c, device


def greet(length, p, device, y, x, c):
    barrier = pltpu.get_barrier_semaphore()
    for other in (device(c=1 - c), device(x=1 - x), device(y=1 - y)):
        pl.semaphore_signal(barrier, inc=1, device_id=(other,), device_id_type=MESH)
    sides = ((-1, p > 0), (1, p < length - 1)) if length > 1 else ()
    for dz, there in sides:
        @pl.when(there)
        def _():
            pl.semaphore_signal(barrier, inc=1, device_id=(device(dz),), device_id_type=MESH)
    peers = 3
    for _, there in sides:
        peers = peers + there.astype(jnp.int32)
    pl.semaphore_wait(barrier, peers)


def gather_body(length, x_ref, o_ref, send_sem, recv_sem, own_sem):
    p, y, x, c, device = place(length)
    greet(length, p, device, y, x, c)

    def block(h, z, yy, xx, cc):
        return o_ref.at[z, yy, xx, cc, h]

    def code(h, z, yy, xx, cc):
        return h * (8 * length) + ((z * 2 + yy) * 2 + xx) * 2 + cc

    def copy(src, h, where, slot, target):
        return pltpu.make_async_remote_copy(
            src_ref=src,
            dst_ref=block(h, *where),
            send_sem=send_sem.at[slot],
            recv_sem=recv_sem.at[code(h, *where)],
            device_id=(target,),
            device_id_type=MESH,
        )

    def arrived(h, where):
        copy(block(h, *where), h, where, 0, device(c=1 - c)).wait_recv()

    per_half = 9 * length
    started = []

    def send(src, h, where, slot, target, there=None):
        made = copy(src, h, where, h * per_half + slot, target)
        if there is None:
            made.start()
        else:
            pl.when(there)(made.start)
        started.append((made, there))

    own = [pltpu.make_async_copy(x_ref.at[h], block(h, p, y, x, c), own_sem.at[h]) for h in range(2)]
    for h in range(2):
        own[h].start()

    if length == 4:
        order = [
            p,
            jnp.where(p == 0, 1, p - 1),
            jnp.where(p == 0, 2, jnp.where(p == 3, 1, p + 1)),
            jnp.where(p < 2, 3, 0),
        ]
    else:
        order = [p]

    def sides(h, z):
        first = (z, 1 - y, x, c) if h == 0 else (z, y, 1 - x, c)
        seconds = (
            [(z, y, 1 - x, c), (z, 1 - y, 1 - x, c)]
            if h == 0
            else [(z, 1 - y, x, c), (z, 1 - y, 1 - x, c)]
        )
        first_to = device(y=1 - y) if h == 0 else device(x=1 - x)
        second_to = device(x=1 - x) if h == 0 else device(y=1 - y)
        return first, seconds, first_to, second_to

    def stage_z(j):
        z = order[j]
        for h in range(2):
            where = (z, y, x, c)
            if j:
                arrived(h, where)
            src = block(h, *where) if j else x_ref.at[h]
            if length > 1:
                right = (p < length - 1) & (z <= p)
                left = (p > 0) & (z >= p)
                send(src, h, where, 9 * j, device(1), right)
                send(src, h, where, 9 * j + 1, device(-1), left)
            _, _, first_to, second_to = sides(h, z)
            send(src, h, where, 9 * j + 2, first_to)
            send(src, h, where, 9 * j + 3, second_to)
            send(src, h, where, 9 * j + 4, device(c=1 - c))

    def stage_first(j):
        z = order[j]
        for h in range(2):
            first, _, _, second_to = sides(h, z)
            arrived(h, first)
            send(block(h, *first), h, first, 9 * j + 5, second_to)
            send(block(h, *first), h, first, 9 * j + 6, device(c=1 - c))

    def stage_second(j):
        z = order[j]
        for i in range(2):
            for h in range(2):
                _, seconds, _, _ = sides(h, z)
                arrived(h, seconds[i])
                send(block(h, *seconds[i]), h, seconds[i], 9 * j + 7 + i, device(c=1 - c))

    stage_z(0)
    for j in range(length):
        if j + 1 < length:
            stage_z(j + 1)
        stage_first(j)
        if j:
            stage_second(j - 1)
    stage_second(length - 1)
    for j in range(length):
        for h in range(2):
            for yy, xx in ((y, x), (1 - y, x), (y, 1 - x), (1 - y, 1 - x)):
                arrived(h, (order[j], yy, xx, 1 - c))
    for h in range(2):
        own[h].wait()
    for made, there in started:
        if there is None:
            made.wait_send()
        else:
            pl.when(there)(made.wait_send)


def gather(value, length, collective_id):
    rows, width = value.shape
    half = rows // 2
    out = pl.pallas_call(
        functools.partial(gather_body, length),
        out_shape=jax.ShapeDtypeStruct((length, 2, 2, 2, 2, half, width), value.dtype),
        in_specs=[pl.BlockSpec(memory_space=pltpu.VMEM)],
        out_specs=pl.BlockSpec(memory_space=pl.ANY),
        scratch_shapes=[
            pltpu.SemaphoreType.DMA((18 * length,)),
            pltpu.SemaphoreType.DMA((16 * length,)),
            pltpu.SemaphoreType.DMA((2,)),
        ],
        compiler_params=pltpu.CompilerParams(collective_id=collective_id, has_side_effects=True),
    )(value.reshape(2, half, width))
    return out.reshape(8 * length * rows, width)


def scatter_body(length, in_ref, o_ref, pair_in, near, first_in, second_in, z_in, total,
                 send_sem, pair_sem, load_sem, first_sem, second_sem, z_sem):
    p, y, x, c, device = place(length)
    greet(length, p, device, y, x, c)
    half, width = o_ref.shape[1:]
    order = [3, 0, 2, 1] if length == 4 else [0]
    step = min(16, half)
    started = []

    def part(h, z, far, cc):
        if h == 0:
            return in_ref.at[z, :, (1 - x if far else x), cc, h]
        return in_ref.at[z, (1 - y if far else y), :, cc, h]

    def send(src, dst, slot, sem, target, there=None):
        made = pltpu.make_async_remote_copy(
            src_ref=src, dst_ref=dst, send_sem=send_sem.at[slot], recv_sem=sem,
            device_id=(target,), device_id_type=MESH,
        )
        if there is None:
            made.start()
        else:
            pl.when(there)(made.start)
        started.append((made, there))
        return made

    first_to = (device(x=1 - x), device(y=1 - y))
    second_to = (device(y=1 - y), device(x=1 - x))
    place_s = (y, x)
    slot = lambda h, z, k: (h * length + z) * 6 + k
    pairs, loads, firsts, seconds = {}, {}, {}, {}
    for far in (1, 0):
        for z in order:
            for h in range(2):
                k = (h * length + z) * 2 + far
                pairs[h, z, far] = send(
                    part(h, z, far, 1 - c), pair_in.at[h, z, far], slot(h, z, far),
                    pair_sem.at[k], device(c=1 - c),
                )
                loads[h, z, far] = pltpu.make_async_copy(
                    part(h, z, far, c), near.at[h, z, far], load_sem.at[k]
                )
                loads[h, z, far].start()

    def add(target, sources):
        def body(i, _):
            rows = pl.ds(pl.multiple_of(i * step, step), step)
            value = sources[0][rows, :].astype(FL)
            for source in sources[1:]:
                value = value + source[rows, :].astype(FL)
            target[rows, :] = value.astype(target.dtype)
            return 0
        lax.fori_loop(0, half // step, body, 0)

    def stage_first(z):
        for h in range(2):
            pairs[h, z, 1].wait_recv()
            loads[h, z, 1].wait()
            for s in range(2):
                add(near.at[h, z, 1, s], [near.at[h, z, 1, s], pair_in.at[h, z, 1, s]])
            firsts[h, z] = send(
                near.at[h, z, 1], first_in.at[h, z], slot(h, z, 2),
                first_sem.at[h * length + z], first_to[h],
            )

    def stage_second(z):
        for h in range(2):
            s = 1 - place_s[h]
            pairs[h, z, 0].wait_recv()
            loads[h, z, 0].wait()
            firsts[h, z].wait_recv()
            add(near.at[h, z, 0, s],
                [near.at[h, z, 0, s], pair_in.at[h, z, 0, s], first_in.at[h, z, s]])
            seconds[h, z] = send(
                near.at[h, z, 0, s], second_in.at[h, z], slot(h, z, 3),
                second_sem.at[h * length + z], second_to[h],
            )

    def stage_z(z):
        for h in range(2):
            s = place_s[h]
            seconds[h, z].wait_recv()
            sources = [near.at[h, z, 0, s], pair_in.at[h, z, 0, s], first_in.at[h, z, s],
                       second_in.at[h, z]]
            if length == 1:
                add(o_ref.at[h], sources)
                continue
            add(total.at[h, z], sources)
            for side, sender in ((0, (p > 0) & (p <= z)), (1, (p < length - 1) & (p >= z))):
                @pl.when(sender)
                def _():
                    k = (h * length + z) * 2 + side
                    pltpu.make_async_remote_copy(
                        src_ref=near.at[h, z, 0, s], dst_ref=z_in.at[h, z, side],
                        send_sem=send_sem.at[0], recv_sem=z_sem.at[k],
                        device_id=(device(c=1 - c),), device_id_type=MESH,
                    ).wait_recv()
                    add(total.at[h, z], [total.at[h, z], z_in.at[h, z, side]])
            @pl.when(p == z)
            def _():
                add(o_ref.at[h], [total.at[h, z]])
            @pl.when(p != z)
            def _():
                add(near.at[h, z, 0, s], [total.at[h, z]])
            send(near.at[h, z, 0, s], z_in.at[h, z, 0], slot(h, z, 4),
                 z_sem.at[(h * length + z) * 2], device(1), p < z)
            send(near.at[h, z, 0, s], z_in.at[h, z, 1], slot(h, z, 5),
                 z_sem.at[(h * length + z) * 2 + 1], device(-1), p > z)

    stages = {"f": stage_first, "s": stage_second, "z": stage_z}
    for kind, i in PLAN[length]:
        stages[kind](order[i])
    for made, there in started:
        if there is None:
            made.wait_send()
        else:
            pl.when(there)(made.wait_send)


def scatter(value, length, collective_id):
    rows, width = value.shape[0] // (8 * length), value.shape[1]
    half = rows // 2
    out = pl.pallas_call(
        functools.partial(scatter_body, length),
        out_shape=jax.ShapeDtypeStruct((2, half, width), FL),
        in_specs=[pl.BlockSpec(memory_space=pl.ANY)],
        out_specs=pl.BlockSpec(memory_space=pltpu.VMEM),
        scratch_shapes=[
            pltpu.VMEM((2, length, 2, 2, half, width), value.dtype),
            pltpu.VMEM((2, length, 2, 2, half, width), value.dtype),
            pltpu.VMEM((2, length, 2, half, width), value.dtype),
            pltpu.VMEM((2, length, half, width), value.dtype),
            pltpu.VMEM((2, length, 2, half, width), value.dtype),
            pltpu.VMEM((2, length, half, width), FL),
            pltpu.SemaphoreType.DMA((12 * length,)),
            pltpu.SemaphoreType.DMA((4 * length,)),
            pltpu.SemaphoreType.DMA((4 * length,)),
            pltpu.SemaphoreType.DMA((2 * length,)),
            pltpu.SemaphoreType.DMA((2 * length,)),
            pltpu.SemaphoreType.DMA((4 * length,)),
        ],
        compiler_params=pltpu.CompilerParams(
            collective_id=collective_id, has_side_effects=True, vmem_limit_bytes=50 << 20
        ),
    )(value.reshape(length, 2, 2, 2, 2, half, width))
    return out.reshape(rows, width)


def dot(a, b, dims=((1,), (0,))):
    return lax.dot_general(a, b, (dims, ((), ())), preferred_element_type=FL)


def feed_body(mid_ref, grad_ref, weight_ref, w1_ref, w2_ref, part_ref, out_ref, act_ref, pre_ref,
              *, gate_column, shared_width):
    full = w2_ref.shape[0]
    mid, grad = mid_ref[...], grad_ref[...]
    pre = dot(mid, w1_ref[...])
    grad_act = dot(grad, w2_ref[...], ((1,), (1,)))
    gate_pre, up = pre[:, :full], pre[:, full:]
    shared_scale = jax.nn.sigmoid(gate_pre[:, gate_column : gate_column + 1])
    column = lax.broadcasted_iota(jnp.int32, gate_pre.shape, 1)
    factor = jnp.where(column < shared_width, shared_scale, weight_ref[...])
    sig = jax.nn.sigmoid(gate_pre)
    silu = gate_pre * sig
    act = silu * up
    low = (act * factor).astype(BF)
    logit = jnp.sum(
        act[:, :shared_width] * grad_act[:, :shared_width], axis=1, keepdims=True
    )
    d_logit = logit * shared_scale * (1.0 - shared_scale)
    scaled = grad_act * factor
    d_gate = scaled * up * sig * (1.0 + gate_pre * (1.0 - sig))
    d_gate = jnp.where(column == gate_column, d_logit, d_gate)
    act_ref[...] = low
    pre_ref[:, :full] = d_gate.astype(BF)
    pre_ref[:, full:] = (scaled * silu).astype(BF)
    part_ref[...] = dot(pre_ref[...], w1_ref[...], ((1,), (1,))).astype(BF)
    out_ref[...] = dot(low, w2_ref[...]).astype(BF)


def feed(mid, grad, weight, w1, w2, gate_column, shared_width):
    tokens, width = mid.shape
    full = w2.shape[0]
    block = 256
    row = lambda columns: pl.BlockSpec((block, columns), lambda i: (i, 0))
    whole = lambda shape: pl.BlockSpec(
        shape, lambda i: (0, 0), pipeline_mode=pl.Buffered(buffer_count=1)
    )
    return pl.pallas_call(
        functools.partial(feed_body, gate_column=gate_column, shared_width=shared_width),
        grid=(tokens // block,),
        out_shape=(
            jax.ShapeDtypeStruct((tokens, width), BF),
            jax.ShapeDtypeStruct((tokens, width), BF),
            jax.ShapeDtypeStruct((tokens, full), BF),
            jax.ShapeDtypeStruct((tokens, 2 * full), BF),
        ),
        in_specs=[row(width), row(width), row(1), whole(w1.shape), whole(w2.shape)],
        out_specs=(row(width), row(width), row(full), row(2 * full)),
        compiler_params=pltpu.CompilerParams(vmem_limit_bytes=56 << 20),
        cost_estimate=pl.CostEstimate(
            flops=12 * tokens * width * full, bytes_accessed=12 * tokens * width,
            transcendentals=tokens * full,
        ),
    )(mid, grad, weight, w1, w2)


def rms_norm(vector, factor):
    return vector * lax.rsqrt(jnp.mean(vector * vector, axis=-1, keepdims=True) + EPSILON) * factor


def rotate(vector, cosine, sine):
    middle = vector.shape[-1] // 2
    turned = jnp.concatenate([-vector[..., middle:], vector[..., :middle]], axis=-1)
    return vector * cosine + turned * sine


def unrotate(grad, cosine, sine):
    middle = grad.shape[-1] // 2
    scaled = grad * sine
    turned = jnp.concatenate([scaled[..., middle:], -scaled[..., :middle]], axis=-1)
    return grad * cosine + turned


def pair_weight_table(expert_ids, route_weights, order_row, expert_count, capacity):
    rows, top = expert_ids.shape
    pairs = rows * top
    flat = expert_ids.reshape(pairs)
    index = jnp.arange(pairs, dtype=jnp.int32)
    turn = jnp.sum(
        jnp.where(order_row[None, :] == index[:, None], index[None, :], 0), axis=1, dtype=jnp.int32
    )
    before = (turn[None, :] < turn[:, None]) & (flat[None, :] == flat[:, None])
    slots = jnp.sum(before.astype(jnp.int32), axis=1, dtype=jnp.int32)
    kept = (slots < capacity).astype(FL).reshape(rows, top)
    hit = expert_ids[:, :, None] == jnp.arange(expert_count, dtype=jnp.int32)[None, None, :]
    return jnp.sum(jnp.where(hit, (route_weights * kept)[:, :, None], 0.0), axis=1)


def per_device(
    tokens,
    cotangent,
    segment_ids,
    expert_ids,
    route_weights,
    pair_order,
    norm_in_gain,
    qkv_weight,
    qkv_bias,
    out_weight,
    norm_mid_gain,
    shared_gate,
    shared_in,
    shared_out,
    expert_in,
    expert_out,
):
    rows, width = tokens.shape
    count = lax.axis_size(AXIS)
    me = lax.axis_index(AXIS)
    team = SEQ // rows
    teams = count // team
    slab = me // team
    seat = me % team
    heads = width // HEAD_DIM
    own = heads // team
    span = own * HEAD_DIM
    top = expert_ids.shape[1]
    expert_count = count // EXP_PARTS
    capacity = (9 * rows * top + 8 * expert_count - 1) // (8 * expert_count)
    score_scale = HEAD_DIM ** (-0.5)
    in_team = [[s * team + p for p in range(team)] for s in range(teams)]
    across = [[s * team + p for s in range(teams)] for p in range(team)]
    share = width // count
    bias_share = 3 * width // count
    hid_s = shared_out.shape[0]
    hid_e = expert_out.shape[1]

    layered = team == 8 and teams == 4

    def team_gather(value, call):
        if layered:
            return gather(value, 1, call)
        return lax.all_gather(value, AXIS, axis=0, tiled=True, axis_index_groups=in_team)

    def team_scatter(value, call):
        if layered:
            return scatter(value, 1, call)
        return lax.psum_scatter(
            value, AXIS, scatter_dimension=0, tiled=True, axis_index_groups=in_team
        )

    table = pair_weight_table(expert_ids, route_weights, pair_order[0], expert_count, capacity)
    packed = jnp.concatenate(
        [
            norm_in_gain.astype(FL),
            qkv_bias.astype(FL),
            norm_mid_gain.astype(FL),
            shared_gate.astype(FL),
            segment_ids.astype(FL),
            table.T.reshape(-1),
        ]
    )
    if layered:
        entries = packed.shape[0]
        lanes = -(-entries // 2048) * 128
        packed = jnp.pad(packed, (0, 16 * lanes - entries)).reshape(16, lanes)
        small = gather(packed, teams, 6).reshape(count, 16 * lanes)[:, :entries]
    else:
        small = lax.all_gather(packed[None], AXIS, axis=0, tiled=True)
    edge = share
    gain_in = small[:, :edge].reshape(1, width)
    bias = small[:, edge : edge + bias_share].reshape(3, heads, HEAD_DIM)
    edge += bias_share
    gain_mid = small[:, edge : edge + share].reshape(1, width)
    edge += share
    gate = small[:, edge : edge + share].reshape(1, width)
    edge += share
    ids_all = small[:, edge : edge + rows]
    edge += rows
    tables = small[:, edge:].reshape(count, expert_count, rows)
    expert_weight = lax.dynamic_index_in_dim(tables, me // EXP_PARTS, 1, False).reshape(-1)

    mine = qkv_weight.reshape(share, 3, team, span).transpose(2, 0, 1, 3)
    mine = lax.all_to_all(
        mine.reshape(team, share, 3 * span),
        AXIS,
        split_axis=0,
        concat_axis=0,
        tiled=True,
        axis_index_groups=in_team,
    )
    w_qkv = lax.all_gather(
        mine.reshape(team * share, 3 * span), AXIS, axis=0, tiled=True, axis_index_groups=across
    )
    deal = [(p * teams + s, s * team + p) for s in range(teams) for p in range(team)]
    w_out = lax.all_gather(
        lax.ppermute(out_weight, AXIS, deal),
        AXIS, axis=0, tiled=True, axis_index_groups=across,
    )
    bias_own = lax.dynamic_slice_in_dim(bias, seat * own, own, 1).reshape(1, 3 * span)

    shared_cols = shared_in.reshape(share, 2, count, hid_s).transpose(2, 0, 1, 3)
    w_shared = lax.all_to_all(
        shared_cols.reshape(count, share, 2 * hid_s),
        AXIS,
        split_axis=0,
        concat_axis=0,
        tiled=True,
    ).reshape(width, 2 * hid_s)
    wide_s = -(-(hid_s + 1) // 128) * 128
    wide_e = -(-hid_e // 128) * 128
    full = wide_s + wide_e

    def columns(value, wide):
        return jnp.pad(value, ((0, 0), (0, wide - value.shape[1])))

    gate_side = jnp.concatenate([w_shared[:, :hid_s], gate.reshape(width, 1).astype(BF)], axis=1)
    w1 = jnp.concatenate(
        [
            columns(gate_side, wide_s),
            columns(expert_in[0][:, :hid_e], wide_e),
            columns(w_shared[:, hid_s:], wide_s),
            columns(expert_in[0][:, hid_e:], wide_e),
        ],
        axis=1,
    )
    w2 = jnp.concatenate(
        [
            jnp.pad(shared_out, ((0, wide_s - hid_s), (0, 0))),
            jnp.pad(expert_out[0], ((0, wide_e - hid_e), (0, 0))),
        ],
        axis=0,
    )
    grad_all = lax.all_gather(cotangent, AXIS, axis=0, tiled=True)

    inputs = tokens.astype(FL)
    scale_in = lax.rsqrt(jnp.mean(inputs * inputs, axis=-1, keepdims=True) + EPSILON)
    normed = team_gather((inputs * scale_in * gain_in).astype(BF), 0)
    own_ids = lax.dynamic_slice_in_dim(ids_all, slab * team, team, 0).reshape(SEQ)
    prev_ids = lax.dynamic_slice_in_dim(
        ids_all, jnp.maximum(slab - 1, 0) * team, team, 0
    ).reshape(SEQ)
    key_ids = jnp.concatenate([jnp.where(slab > 0, prev_ids, -1.0), own_ids])
    slot = jnp.arange(SEQ, dtype=jnp.int32)
    earlier = (key_ids[None, :] < own_ids[:, None]).astype(jnp.int32)
    positions = (SEQ + slot - jnp.sum(earlier, axis=1, dtype=jnp.int32)).astype(FL)
    inverse = THETA ** (-jnp.arange(0, HEAD_DIM, 2, dtype=FL) / HEAD_DIM)
    angles = positions[:, None] * inverse[None, :]
    angles = jnp.concatenate([angles, angles], axis=-1)
    cosine = jnp.cos(angles)[:, None, :]
    sine = jnp.sin(angles)[:, None, :]

    projected = dot(normed, w_qkv) + bias_own
    queries = rotate(projected[:, :span].reshape(SEQ, own, HEAD_DIM), cosine, sine).astype(BF)
    keys = rotate(projected[:, span : 2 * span].reshape(SEQ, own, HEAD_DIM), cosine, sine)
    key_value = jnp.stack([keys.astype(BF).reshape(SEQ, span), projected[:, 2 * span :].astype(BF)])
    forward = [(source, source + team) for source in range(count - team)]
    backward = [(target, source) for source, target in forward]
    passed = lax.ppermute(key_value, AXIS, forward)
    window = jnp.concatenate([passed, key_value], axis=1).reshape(2, 2 * SEQ, own, HEAD_DIM)
    allowed = (
        jnp.arange(2 * SEQ, dtype=jnp.int32)[None, :] <= slot[:, None] + SEQ
    ) & (key_ids[None, :] == own_ids[:, None])

    def masked_scores():
        scores = (
            jnp.einsum("qhd,khd->hqk", queries, window[0], preferred_element_type=FL) * score_scale
        )
        return jnp.where(allowed[None], scores, MASKED)

    scores = masked_scores()
    top_score = jnp.max(scores, axis=-1, keepdims=True)
    log_total = top_score + jnp.log(
        jnp.sum(jnp.exp(scores - top_score), axis=-1, keepdims=True)
    )
    probs = jnp.exp(scores - log_total).astype(BF)
    attended = jnp.einsum("hqk,khd->qhd", probs, window[1], preferred_element_type=FL)
    attended = attended.reshape(SEQ, span).astype(BF)
    hidden = inputs + team_scatter(dot(attended, w_out).astype(BF), 1).astype(FL)
    scale_mid = lax.rsqrt(jnp.mean(hidden * hidden, axis=-1, keepdims=True) + EPSILON)
    mid = (hidden * scale_mid * gain_mid).astype(BF)

    if layered:
        mid_all = gather(mid, teams, 2)
    else:
        mid_all = lax.all_gather(mid, AXIS, axis=0, tiled=True)
    mid_part, out_part, act_low, d_pre = feed(
        mid_all, grad_all, expert_weight[:, None], w1, w2, hid_s, wide_s
    )
    if layered:
        summed_mid = scatter(mid_part, teams, 3)
    else:
        summed_mid = lax.psum_scatter(mid_part, AXIS, scatter_dimension=0, tiled=True)
    summed_out = lax.psum_scatter(out_part, AXIS, scatter_dimension=0, tiled=True)
    d_w1 = dot(mid_all, d_pre, ((0,), (0,)))
    d_w2 = dot(act_low, grad_all, ((0,), (0,)))
    shared_out_grad = d_w2[:hid_s]
    expert_out_grad = d_w2[wide_s : wide_s + hid_e]
    expert_in_grad = jnp.concatenate(
        [d_w1[:, wide_s : wide_s + hid_e], d_w1[:, full + wide_s : full + wide_s + hid_e]], axis=1
    )
    d_shared = jnp.concatenate([d_w1[:, :hid_s], d_w1[:, full : full + hid_s]], axis=1)
    gate_grad = d_w1[:, hid_s]
    shared_back = lax.all_to_all(
        d_shared.astype(BF).reshape(count, share, 2 * hid_s),
        AXIS,
        split_axis=0,
        concat_axis=0,
        tiled=True,
    )
    shared_in_grad = (
        shared_back.reshape(count, share, 2, hid_s)
        .transpose(1, 2, 0, 3)
        .reshape(share, -1)
        .astype(FL)
    )
    output = (hidden + summed_out.astype(FL)).astype(BF)

    grad_out = cotangent.astype(FL)
    d_mid = summed_mid.astype(FL)

    def norm_back(value, scale, gain, grad):
        unit = value * scale
        weighted = grad * gain
        inner = jnp.mean(weighted * unit, axis=-1, keepdims=True)
        return scale * (weighted - unit * inner), jnp.sum(grad * unit, axis=0)

    d_hidden_part, gain_mid_grad = norm_back(hidden, scale_mid, gain_mid, d_mid)
    d_hidden = grad_out + d_hidden_part
    d_attn = team_gather(d_hidden.astype(BF), 4)
    d_attended = dot(d_attn, w_out, ((1,), (1,))).astype(BF)
    out_grad = dot(attended, d_attn, ((0,), (0,)))
    d_attended = d_attended.reshape(SEQ, own, HEAD_DIM)
    attention = jnp.exp(masked_scores() - log_total)
    d_attention = jnp.einsum("qhd,khd->hqk", d_attended, window[1], preferred_element_type=FL)
    row_delta = jnp.sum(attention * d_attention, axis=-1, keepdims=True)
    d_scores = (attention * (d_attention - row_delta)).astype(BF)
    d_queries = (
        jnp.einsum("hqk,khd->qhd", d_scores, window[0], preferred_element_type=FL) * score_scale
    )
    d_keys = jnp.einsum("hqk,qhd->khd", d_scores, queries, preferred_element_type=FL) * score_scale
    d_values = jnp.einsum(
        "hqk,qhd->khd", attention.astype(BF), d_attended, preferred_element_type=FL
    )
    d_kv = jnp.stack([d_keys.reshape(2 * SEQ, span), d_values.reshape(2 * SEQ, span)])
    returned = lax.ppermute(d_kv[:, :SEQ].astype(BF), AXIS, backward).astype(FL)
    d_kv = d_kv[:, SEQ:] + returned
    d_projected = jnp.concatenate(
        [
            unrotate(d_queries, cosine, sine).reshape(SEQ, span),
            unrotate(d_kv[0].reshape(SEQ, own, HEAD_DIM), cosine, sine).reshape(SEQ, span),
            d_kv[1],
        ],
        axis=1,
    ).astype(BF)
    d_normed = team_scatter(dot(d_projected, w_qkv, ((1,), (1,))).astype(BF), 5).astype(FL)
    d_inputs, gain_in_grad = norm_back(inputs, scale_in, gain_in, d_normed)
    input_grad = d_hidden + d_inputs
    qkv_grad = dot(normed, d_projected, ((0,), (0,)))
    bias_grad = jnp.sum(d_projected.astype(FL), axis=0).reshape(3, own, HEAD_DIM)

    qkv_part = lax.psum_scatter(
        qkv_grad.astype(BF), AXIS, scatter_dimension=0, tiled=True, axis_index_groups=across
    )
    qkv_part = lax.all_to_all(
        qkv_part.reshape(team, share, 3 * span),
        AXIS,
        split_axis=0,
        concat_axis=0,
        tiled=True,
        axis_index_groups=in_team,
    )
    qkv_weight_grad = (
        qkv_part.reshape(team, share, 3, span)
        .transpose(1, 2, 0, 3)
        .reshape(share, 3 * width)
        .astype(FL)
    )
    out_part_grad = lax.psum_scatter(
        out_grad.astype(BF), AXIS, scatter_dimension=0, tiled=True, axis_index_groups=across
    )
    out_weight_grad = lax.ppermute(
        out_part_grad, AXIS, [(target, source) for source, target in deal]
    ).astype(FL)
    bias_spread = lax.dynamic_update_slice_in_dim(
        jnp.zeros((3, heads, HEAD_DIM), FL), bias_grad, seat * own, 1
    )
    small_grads = jnp.concatenate(
        [
            gain_in_grad.reshape(count, share),
            bias_spread.reshape(count, bias_share),
            gain_mid_grad.reshape(count, share),
            gate_grad.reshape(count, share),
        ],
        axis=1,
    )
    if layered:
        entries = small_grads.shape[1]
        lanes = -(-entries // 2048) * 128
        small_grads = jnp.pad(small_grads, ((0, 0), (0, 16 * lanes - entries)))
        small_sum = scatter(small_grads.reshape(count * 16, lanes), teams, 7).reshape(-1)[:entries]
    else:
        small_sum = lax.psum_scatter(small_grads, AXIS, scatter_dimension=0, tiled=True)[0]
    return (
        output,
        input_grad,
        small_sum[:share],
        qkv_weight_grad,
        small_sum[share : share + bias_share],
        out_weight_grad,
        small_sum[share + bias_share : 2 * share + bias_share],
        small_sum[2 * share + bias_share :],
        shared_in_grad,
        shared_out_grad,
        expert_in_grad[None],
        expert_out_grad[None],
    )


def solution(mesh):
    row, flat, deep = P("fsdp", None), P("fsdp"), P("fsdp", None, None)
    return jax.shard_map(
        per_device,
        mesh=mesh,
        in_specs=(
            row, row, flat, row, row, row, flat, row, flat, row, flat, flat, row, row, deep, deep,
        ),
        out_specs=(row, row, flat, row, flat, row, flat, flat, row, row, deep, deep),
        check_vma=False,
    )
```

```python
import functools

import jax
import jax.numpy as jnp
from jax import lax
from jax.experimental import pallas as pl
from jax.experimental.pallas import tpu as pltpu
from jax.sharding import PartitionSpec as P

HEAD_DIM = 128
EXP_PARTS = 4
SEQ = 1024

EPSILON = 1e-06
THETA = 1000000.0
MASKED = -1e30
BF = jnp.bfloat16
FL = jnp.float32
AXIS = "fsdp"
MESH = pl.DeviceIdType.MESH


def place(length):
    me = lax.axis_index(AXIS)
    z, y, x, c = me // 8, (me // 4) % 2, (me // 2) % 2, me % 2

    def device(dz=0, y=y, x=x, c=c):
        return (((z + dz) * 2 + y) * 2 + x) * 2 + c

    return (z if length > 1 else z * 0), y, x, c, device


def greet(length, p, device, y, x, c):
    barrier = pltpu.get_barrier_semaphore()
    for other in (device(c=1 - c), device(x=1 - x), device(y=1 - y)):
        pl.semaphore_signal(barrier, inc=1, device_id=(other,), device_id_type=MESH)
    sides = ((-1, p > 0), (1, p < length - 1)) if length > 1 else ()
    for dz, there in sides:
        @pl.when(there)
        def _():
            pl.semaphore_signal(barrier, inc=1, device_id=(device(dz),), device_id_type=MESH)
    peers = 3
    for _, there in sides:
        peers = peers + there.astype(jnp.int32)
    pl.semaphore_wait(barrier, peers)


def line_order(p):
    return [
        p,
        jnp.where(p == 0, 1, p - 1),
        jnp.where(p == 0, 2, jnp.where(p == 3, 1, p + 1)),
        jnp.where(p < 2, 3, 0),
    ]


def gather_body(length, x_ref, o_ref, send_sem, recv_sem, own_sem, line=None):
    p, y, x, c, device = place(length)
    if line is None:
        greet(length, p, device, y, x, c)
        line = [lambda: None] * 5

    def block(h, z, yy, xx, cc):
        return o_ref.at[z, yy, xx, cc, h]

    def code(h, z, yy, xx, cc):
        return h * (8 * length) + ((z * 2 + yy) * 2 + xx) * 2 + cc

    def copy(src, h, where, slot, target):
        return pltpu.make_async_remote_copy(
            src_ref=src,
            dst_ref=block(h, *where),
            send_sem=send_sem.at[slot],
            recv_sem=recv_sem.at[code(h, *where)],
            device_id=(target,),
            device_id_type=MESH,
        )

    def arrived(h, where):
        copy(block(h, *where), h, where, 0, device(c=1 - c)).wait_recv()

    per_half = 9 * length
    started = []

    def send(src, h, where, slot, target, there=None):
        made = copy(src, h, where, h * per_half + slot, target)
        if there is None:
            made.start()
        else:
            pl.when(there)(made.start)
        started.append((made, there))

    own = [pltpu.make_async_copy(x_ref.at[h], block(h, p, y, x, c), own_sem.at[h]) for h in range(2)]
    for h in range(2):
        own[h].start()

    if length == 4:
        order = line_order(p)
    else:
        order = [p]

    def sides(h, z):
        first = (z, 1 - y, x, c) if h == 0 else (z, y, 1 - x, c)
        seconds = (
            [(z, y, 1 - x, c), (z, 1 - y, 1 - x, c)]
            if h == 0
            else [(z, 1 - y, x, c), (z, 1 - y, 1 - x, c)]
        )
        first_to = device(y=1 - y) if h == 0 else device(x=1 - x)
        second_to = device(x=1 - x) if h == 0 else device(y=1 - y)
        return first, seconds, first_to, second_to

    def stage_z(j):
        z = order[j]
        for h in range(2):
            where = (z, y, x, c)
            if j:
                arrived(h, where)
            src = block(h, *where) if j else x_ref.at[h]
            if length > 1:
                right = (p < length - 1) & (z <= p)
                left = (p > 0) & (z >= p)
                send(src, h, where, 9 * j, device(1), right)
                send(src, h, where, 9 * j + 1, device(-1), left)
            _, _, first_to, second_to = sides(h, z)
            send(src, h, where, 9 * j + 2, first_to)
            send(src, h, where, 9 * j + 3, second_to)
            send(src, h, where, 9 * j + 4, device(c=1 - c))

    def stage_first(j):
        z = order[j]
        for h in range(2):
            first, _, _, second_to = sides(h, z)
            arrived(h, first)
            send(block(h, *first), h, first, 9 * j + 5, second_to)
            send(block(h, *first), h, first, 9 * j + 6, device(c=1 - c))

    def stage_second(j):
        z = order[j]
        for i in range(2):
            for h in range(2):
                _, seconds, _, _ = sides(h, z)
                arrived(h, seconds[i])
                send(block(h, *seconds[i]), h, seconds[i], 9 * j + 7 + i, device(c=1 - c))

    line[0]()
    stage_z(0)
    for j in range(length):
        if j + 1 < length:
            stage_z(j + 1)
        stage_first(j)
        if j:
            stage_second(j - 1)
    stage_second(length - 1)
    line[1]()
    for j in range(length):
        for h in range(2):
            for yy, xx in ((y, x), (1 - y, x), (y, 1 - x), (1 - y, 1 - x)):
                arrived(h, (order[j], yy, xx, 1 - c))
    for h in range(2):
        own[h].wait()
    for step in line[2:]:
        step()
    for made, there in started:
        if there is None:
            made.wait_send()
        else:
            pl.when(there)(made.wait_send)


def gather(value, length, collective_id):
    rows, width = value.shape
    half = rows // 2
    out = pl.pallas_call(
        functools.partial(gather_body, length),
        out_shape=jax.ShapeDtypeStruct((length, 2, 2, 2, 2, half, width), value.dtype),
        in_specs=[pl.BlockSpec(memory_space=pltpu.VMEM)],
        out_specs=pl.BlockSpec(memory_space=pl.ANY),
        scratch_shapes=[
            pltpu.SemaphoreType.DMA((18 * length,)),
            pltpu.SemaphoreType.DMA((16 * length,)),
            pltpu.SemaphoreType.DMA((2,)),
        ],
        compiler_params=pltpu.CompilerParams(collective_id=collective_id, has_side_effects=True),
    )(value.reshape(2, half, width))
    return out.reshape(8 * length * rows, width)


def layer_and_line_body(many, *refs):
    x_ref, ins = refs[0], refs[1 : 1 + many]
    o_ref, outs = refs[1 + many], refs[2 + many : 2 + 2 * many]
    send_sem, recv_sem, own_sem, line_send, line_recv, line_own = refs[2 + 2 * many :]
    p, y, x, c, device = place(4)
    greet(4, p, device, y, x, c)
    order = line_order(p)
    started = []
    own = [pltpu.make_async_copy(ins[k], outs[k].at[p], line_own.at[k]) for k in range(many)]

    def copy(k, j, z, side):
        return pltpu.make_async_remote_copy(
            src_ref=outs[k].at[z] if j else ins[k],
            dst_ref=outs[k].at[z],
            send_sem=line_send.at[(k * 4 + j) * 2 + side],
            recv_sem=line_recv.at[k * 4 + z],
            device_id=(device(1 - 2 * side),),
            device_id_type=MESH,
        )

    def stage(j):
        z = order[j]
        for k in range(many):
            if j:
                pltpu.make_async_remote_copy(
                    src_ref=outs[k].at[z], dst_ref=outs[k].at[z], send_sem=line_send.at[0],
                    recv_sem=line_recv.at[k * 4 + z], device_id=(device(c=1 - c),),
                    device_id_type=MESH,
                ).wait_recv()
            else:
                own[k].start()
            for side, there in ((0, (p < 3) & (z <= p)), (1, (p > 0) & (z >= p))):
                made = copy(k, j, z, side)
                pl.when(there)(made.start)
                started.append((made, there))

    def finish():
        for k in range(many):
            own[k].wait()
        for made, there in started:
            pl.when(there)(made.wait_send)

    line = [functools.partial(stage, j) for j in range(4)] + [finish]
    gather_body(1, x_ref, o_ref, send_sem, recv_sem, own_sem, line)


def layer_and_line(value, others, collective_id):
    rows, width = value.shape
    half = rows // 2
    many = len(others)
    outs = pl.pallas_call(
        functools.partial(layer_and_line_body, many),
        out_shape=[jax.ShapeDtypeStruct((1, 2, 2, 2, 2, half, width), value.dtype)]
        + [jax.ShapeDtypeStruct((4,) + other.shape, other.dtype) for other in others],
        in_specs=[pl.BlockSpec(memory_space=pltpu.VMEM)] * (1 + many),
        out_specs=[pl.BlockSpec(memory_space=pl.ANY)] * (1 + many),
        scratch_shapes=[
            pltpu.SemaphoreType.DMA((18,)),
            pltpu.SemaphoreType.DMA((16,)),
            pltpu.SemaphoreType.DMA((2,)),
            pltpu.SemaphoreType.DMA((8 * many,)),
            pltpu.SemaphoreType.DMA((4 * many,)),
            pltpu.SemaphoreType.DMA((many,)),
        ],
        compiler_params=pltpu.CompilerParams(collective_id=collective_id, has_side_effects=True),
    )(value.reshape(2, half, width), *others)
    return [outs[0].reshape(8 * rows, width)] + [
        out.reshape((-1,) + out.shape[2:]) for out in outs[1:]
    ]


def scatter_body(length, many, *refs):
    in_refs, o_refs = refs[:many], refs[many : 2 * many]
    (pair_in, near, first_in, second_in, z_in, total,
     send_sem, pair_sem, load_sem, first_sem, second_sem, z_sem) = refs[2 * many :]
    p, y, x, c, device = place(length)
    greet(length, p, device, y, x, c)
    half, width = total.shape
    order = [3, 0, 2, 1] if length == 4 else [0]
    row_step = min(16, half)
    started = []

    def part(g, z, far, cc):
        if g % 2 == 0:
            return in_refs[g // 2].at[z, :, (1 - x if far else x), cc, 0]
        return in_refs[g // 2].at[z, (1 - y if far else y), :, cc, 1]

    def send(src, dst, slot, sem, target, there=None):
        made = pltpu.make_async_remote_copy(
            src_ref=src, dst_ref=dst, send_sem=send_sem.at[slot], recv_sem=sem,
            device_id=(target,), device_id_type=MESH,
        )
        if there is None:
            made.start()
        else:
            pl.when(there)(made.start)
        started.append((made, there))
        return made

    first_to = (device(x=1 - x), device(y=1 - y))
    second_to = (device(y=1 - y), device(x=1 - x))
    place_s = (y, x)
    slot = lambda g, z, k: (g * length + z) * 6 + k
    pairs, loads, firsts, seconds = {}, {}, {}, {}
    steps = [(q, z) for q in range(many) for z in order]
    for q in range(many):
        for far in (1, 0):
            for z in order:
                for g in (2 * q, 2 * q + 1):
                    k = (g * length + z) * 2 + far
                    pairs[g, z, far] = send(
                        part(g, z, far, 1 - c), pair_in.at[g, z, far], slot(g, z, far),
                        pair_sem.at[k], device(c=1 - c),
                    )
                    loads[g, z, far] = pltpu.make_async_copy(
                        part(g, z, far, c), near.at[g, z, far], load_sem.at[k]
                    )
                    loads[g, z, far].start()

    def add(target, sources):
        def body(i, _):
            rows = pl.ds(pl.multiple_of(i * row_step, row_step), row_step)
            value = sources[0][rows, :].astype(FL)
            for source in sources[1:]:
                value = value + source[rows, :].astype(FL)
            target[rows, :] = value.astype(target.dtype)
            return 0
        lax.fori_loop(0, half // row_step, body, 0)

    def stage_first(q, z):
        for g in (2 * q, 2 * q + 1):
            pairs[g, z, 1].wait_recv()
            loads[g, z, 1].wait()
            for s in range(2):
                add(near.at[g, z, 1, s], [near.at[g, z, 1, s], pair_in.at[g, z, 1, s]])
            firsts[g, z] = send(
                near.at[g, z, 1], first_in.at[g, z], slot(g, z, 2),
                first_sem.at[g * length + z], first_to[g % 2],
            )

    def stage_second(q, z):
        for g in (2 * q, 2 * q + 1):
            s = 1 - place_s[g % 2]
            pairs[g, z, 0].wait_recv()
            loads[g, z, 0].wait()
            firsts[g, z].wait_recv()
            add(near.at[g, z, 0, s],
                [near.at[g, z, 0, s], pair_in.at[g, z, 0, s], first_in.at[g, z, s]])
            seconds[g, z] = send(
                near.at[g, z, 0, s], second_in.at[g, z], slot(g, z, 3),
                second_sem.at[g * length + z], second_to[g % 2],
            )

    def stage_z(q, z):
        for g in (2 * q, 2 * q + 1):
            s = place_s[g % 2]
            o_half = o_refs[q].at[g % 2]
            seconds[g, z].wait_recv()
            sources = [near.at[g, z, 0, s], pair_in.at[g, z, 0, s], first_in.at[g, z, s],
                       second_in.at[g, z]]
            if length == 1:
                add(o_half, sources)
                continue
            add(total, sources)
            for side, sender in ((0, (p > 0) & (p <= z)), (1, (p < length - 1) & (p >= z))):
                @pl.when(sender)
                def _():
                    k = (g * length + z) * 2 + side
                    pltpu.make_async_remote_copy(
                        src_ref=near.at[g, z, 0, s], dst_ref=z_in.at[g, z, side],
                        send_sem=send_sem.at[0], recv_sem=z_sem.at[k],
                        device_id=(device(c=1 - c),), device_id_type=MESH,
                    ).wait_recv()
                    add(total, [total, z_in.at[g, z, side]])
            @pl.when(p == z)
            def _():
                add(o_half, [total])
            @pl.when(p != z)
            def _():
                add(near.at[g, z, 0, s], [total])
            send(near.at[g, z, 0, s], z_in.at[g, z, 0], slot(g, z, 4),
                 z_sem.at[(g * length + z) * 2], device(1), p < z)
            send(near.at[g, z, 0, s], z_in.at[g, z, 1], slot(g, z, 5),
                 z_sem.at[(g * length + z) * 2 + 1], device(-1), p > z)

    count = len(steps)
    for i in range(count + 3):
        for stage, j in ((stage_first, i), (stage_z, i - 3), (stage_second, i - 1)):
            if 0 <= j < count:
                stage(*steps[j])
    for made, there in started:
        if there is None:
            made.wait_send()
        else:
            pl.when(there)(made.wait_send)


def scatter(values, length, collective_id):
    many = len(values)
    rows, width = values[0].shape[0] // (8 * length), values[0].shape[1]
    half = rows // 2
    kind = values[0].dtype
    lanes = 2 * many
    outs = pl.pallas_call(
        functools.partial(scatter_body, length, many),
        out_shape=[jax.ShapeDtypeStruct((2, half, width), FL)] * many,
        in_specs=[pl.BlockSpec(memory_space=pl.ANY)] * many,
        out_specs=[pl.BlockSpec(memory_space=pltpu.VMEM)] * many,
        scratch_shapes=[
            pltpu.VMEM((lanes, length, 2, 2, half, width), kind),
            pltpu.VMEM((lanes, length, 2, 2, half, width), kind),
            pltpu.VMEM((lanes, length, 2, half, width), kind),
            pltpu.VMEM((lanes, length, half, width), kind),
            pltpu.VMEM((lanes, length, 2, half, width), kind),
            pltpu.VMEM((half, width), FL),
            pltpu.SemaphoreType.DMA((6 * lanes * length,)),
            pltpu.SemaphoreType.DMA((2 * lanes * length,)),
            pltpu.SemaphoreType.DMA((2 * lanes * length,)),
            pltpu.SemaphoreType.DMA((lanes * length,)),
            pltpu.SemaphoreType.DMA((lanes * length,)),
            pltpu.SemaphoreType.DMA((2 * lanes * length,)),
        ],
        compiler_params=pltpu.CompilerParams(
            collective_id=collective_id, has_side_effects=True, vmem_limit_bytes=62 << 20
        ),
    )(*[value.reshape(length, 2, 2, 2, 2, half, width) for value in values])
    return [out.reshape(rows, width) for out in outs]


def dot(a, b, dims=((1,), (0,))):
    return lax.dot_general(a, b, (dims, ((), ())), preferred_element_type=FL)


def feed_body(mid_ref, grad_ref, weight_ref, w1_ref, w2_ref, part_ref, out_ref, act_ref, pre_ref,
              *, gate_column, shared_width):
    full = w2_ref.shape[0]
    mid, grad = mid_ref[...], grad_ref[...]
    pre = dot(mid, w1_ref[...])
    grad_act = dot(grad, w2_ref[...], ((1,), (1,)))
    gate_pre, up = pre[:, :full], pre[:, full:]
    shared_scale = jax.nn.sigmoid(gate_pre[:, gate_column : gate_column + 1])
    column = lax.broadcasted_iota(jnp.int32, gate_pre.shape, 1)
    factor = jnp.where(column < shared_width, shared_scale, weight_ref[...])
    sig = jax.nn.sigmoid(gate_pre)
    silu = gate_pre * sig
    act = silu * up
    low = (act * factor).astype(BF)
    logit = jnp.sum(
        act[:, :shared_width] * grad_act[:, :shared_width], axis=1, keepdims=True
    )
    d_logit = logit * shared_scale * (1.0 - shared_scale)
    scaled = grad_act * factor
    d_gate = scaled * up * sig * (1.0 + gate_pre * (1.0 - sig))
    d_gate = jnp.where(column == gate_column, d_logit, d_gate)
    act_ref[...] = low
    pre_ref[:, :full] = d_gate.astype(BF)
    pre_ref[:, full:] = (scaled * silu).astype(BF)
    part_ref[...] = dot(pre_ref[...], w1_ref[...], ((1,), (1,))).astype(BF)
    out_ref[...] = dot(low, w2_ref[...]).astype(BF)


def feed(mid, grad, weight, w1, w2, gate_column, shared_width):
    tokens, width = mid.shape
    full = w2.shape[0]
    block = 256
    row = lambda columns: pl.BlockSpec((block, columns), lambda i: (i, 0))
    whole = lambda shape: pl.BlockSpec(
        shape, lambda i: (0, 0), pipeline_mode=pl.Buffered(buffer_count=1)
    )
    return pl.pallas_call(
        functools.partial(feed_body, gate_column=gate_column, shared_width=shared_width),
        grid=(tokens // block,),
        out_shape=(
            jax.ShapeDtypeStruct((tokens, width), BF),
            jax.ShapeDtypeStruct((tokens, width), BF),
            jax.ShapeDtypeStruct((tokens, full), BF),
            jax.ShapeDtypeStruct((tokens, 2 * full), BF),
        ),
        in_specs=[row(width), row(width), row(1), whole(w1.shape), whole(w2.shape)],
        out_specs=(row(width), row(width), row(full), row(2 * full)),
        compiler_params=pltpu.CompilerParams(vmem_limit_bytes=56 << 20),
        cost_estimate=pl.CostEstimate(
            flops=12 * tokens * width * full, bytes_accessed=12 * tokens * width,
            transcendentals=tokens * full,
        ),
    )(mid, grad, weight, w1, w2)


def rms_norm(vector, factor):
    return vector * lax.rsqrt(jnp.mean(vector * vector, axis=-1, keepdims=True) + EPSILON) * factor


def rotate(vector, cosine, sine):
    middle = vector.shape[-1] // 2
    turned = jnp.concatenate([-vector[..., middle:], vector[..., :middle]], axis=-1)
    return vector * cosine + turned * sine


def unrotate(grad, cosine, sine):
    middle = grad.shape[-1] // 2
    scaled = grad * sine
    turned = jnp.concatenate([scaled[..., middle:], -scaled[..., :middle]], axis=-1)
    return grad * cosine + turned


def pair_weight_table(expert_ids, route_weights, order_row, expert_count, capacity):
    rows, top = expert_ids.shape
    pairs = rows * top
    flat = expert_ids.reshape(pairs)
    index = jnp.arange(pairs, dtype=jnp.int32)
    turn = jnp.sum(
        jnp.where(order_row[None, :] == index[:, None], index[None, :], 0), axis=1, dtype=jnp.int32
    )
    before = (turn[None, :] < turn[:, None]) & (flat[None, :] == flat[:, None])
    slots = jnp.sum(before.astype(jnp.int32), axis=1, dtype=jnp.int32)
    kept = (slots < capacity).astype(FL).reshape(rows, top)
    hit = expert_ids[:, :, None] == jnp.arange(expert_count, dtype=jnp.int32)[None, None, :]
    return jnp.sum(jnp.where(hit, (route_weights * kept)[:, :, None], 0.0), axis=1)


def per_device(
    tokens,
    cotangent,
    segment_ids,
    expert_ids,
    route_weights,
    pair_order,
    norm_in_gain,
    qkv_weight,
    qkv_bias,
    out_weight,
    norm_mid_gain,
    shared_gate,
    shared_in,
    shared_out,
    expert_in,
    expert_out,
):
    rows, width = tokens.shape
    count = lax.axis_size(AXIS)
    me = lax.axis_index(AXIS)
    team = SEQ // rows
    teams = count // team
    slab = me // team
    seat = me % team
    heads = width // HEAD_DIM
    own = heads // team
    span = own * HEAD_DIM
    top = expert_ids.shape[1]
    expert_count = count // EXP_PARTS
    capacity = (9 * rows * top + 8 * expert_count - 1) // (8 * expert_count)
    score_scale = HEAD_DIM ** (-0.5)
    in_team = [[s * team + p for p in range(team)] for s in range(teams)]
    across = [[s * team + p for s in range(teams)] for p in range(team)]
    share = width // count
    bias_share = 3 * width // count
    hid_s = shared_out.shape[0]
    hid_e = expert_out.shape[1]

    layered = team == 8 and teams == 4

    def team_gather(value, call):
        if layered:
            return gather(value, 1, call)
        return lax.all_gather(value, AXIS, axis=0, tiled=True, axis_index_groups=in_team)

    def team_scatter(value, call):
        if layered:
            return scatter([value], 1, call)[0]
        return lax.psum_scatter(
            value, AXIS, scatter_dimension=0, tiled=True, axis_index_groups=in_team
        )

    table = pair_weight_table(expert_ids, route_weights, pair_order[0], expert_count, capacity)
    packed = jnp.concatenate(
        [
            norm_in_gain.astype(FL),
            qkv_bias.astype(FL),
            norm_mid_gain.astype(FL),
            shared_gate.astype(FL),
            segment_ids.astype(FL),
            table.T.reshape(-1),
        ]
    )
    if layered:
        entries = packed.shape[0]
        lanes = -(-entries // 2048) * 128
        packed = jnp.pad(packed, (0, 16 * lanes - entries)).reshape(16, lanes)
        small = gather(packed, teams, 6).reshape(count, 16 * lanes)[:, :entries]
    else:
        small = lax.all_gather(packed[None], AXIS, axis=0, tiled=True)
    qkv_weight, small = lax.optimization_barrier((qkv_weight, small))
    edge = share
    gain_in = small[:, :edge].reshape(1, width)
    bias = small[:, edge : edge + bias_share].reshape(3, heads, HEAD_DIM)
    edge += bias_share
    gain_mid = small[:, edge : edge + share].reshape(1, width)
    edge += share
    gate = small[:, edge : edge + share].reshape(1, width)
    edge += share
    ids_all = small[:, edge : edge + rows]
    edge += rows
    tables = small[:, edge:].reshape(count, expert_count, rows)
    expert_weight = lax.dynamic_index_in_dim(tables, me // EXP_PARTS, 1, False).reshape(-1)

    mine = qkv_weight.reshape(share, 3, team, span).transpose(2, 0, 1, 3)
    mine = lax.all_to_all(
        mine.reshape(team, share, 3 * span),
        AXIS,
        split_axis=0,
        concat_axis=0,
        tiled=True,
        axis_index_groups=in_team,
    )
    deal = [(p * teams + s, s * team + p) for s in range(teams) for p in range(team)]
    mine = mine.reshape(team * share, 3 * span)
    out_rows = lax.ppermute(out_weight, AXIS, deal)
    inputs = tokens.astype(FL)
    scale_in = lax.rsqrt(jnp.mean(inputs * inputs, axis=-1, keepdims=True) + EPSILON)
    normed = (inputs * scale_in * gain_in).astype(BF)
    if layered:
        normed, w_qkv, w_out = layer_and_line(normed, [mine, out_rows], 0)
    else:
        normed = team_gather(normed, 0)
        w_qkv, w_out = [
            lax.all_gather(value, AXIS, axis=0, tiled=True, axis_index_groups=across)
            for value in (mine, out_rows)
        ]
    bias_own = lax.dynamic_slice_in_dim(bias, seat * own, own, 1).reshape(1, 3 * span)

    shared_in, normed = lax.optimization_barrier((shared_in, normed))

    shared_cols = shared_in.reshape(share, 2, count, hid_s).transpose(2, 0, 1, 3)
    w_shared = lax.all_to_all(
        shared_cols.reshape(count, share, 2 * hid_s),
        AXIS,
        split_axis=0,
        concat_axis=0,
        tiled=True,
    ).reshape(width, 2 * hid_s)
    grad_all = lax.all_gather(cotangent, AXIS, axis=0, tiled=True)

    own_ids = lax.dynamic_slice_in_dim(ids_all, slab * team, team, 0).reshape(SEQ)
    prev_ids = lax.dynamic_slice_in_dim(
        ids_all, jnp.maximum(slab - 1, 0) * team, team, 0
    ).reshape(SEQ)
    key_ids = jnp.concatenate([jnp.where(slab > 0, prev_ids, -1.0), own_ids])
    slot = jnp.arange(SEQ, dtype=jnp.int32)
    earlier = (key_ids[None, :] < own_ids[:, None]).astype(jnp.int32)
    positions = (SEQ + slot - jnp.sum(earlier, axis=1, dtype=jnp.int32)).astype(FL)
    inverse = THETA ** (-jnp.arange(0, HEAD_DIM, 2, dtype=FL) / HEAD_DIM)
    angles = positions[:, None] * inverse[None, :]
    angles = jnp.concatenate([angles, angles], axis=-1)
    cosine = jnp.cos(angles)[:, None, :]
    sine = jnp.sin(angles)[:, None, :]

    projected = dot(normed, w_qkv) + bias_own
    queries = rotate(projected[:, :span].reshape(SEQ, own, HEAD_DIM), cosine, sine).astype(BF)
    keys = rotate(projected[:, span : 2 * span].reshape(SEQ, own, HEAD_DIM), cosine, sine)
    key_value = jnp.stack([keys.astype(BF).reshape(SEQ, span), projected[:, 2 * span :].astype(BF)])
    forward = [(source, source + team) for source in range(count - team)]
    backward = [(target, source) for source, target in forward]
    passed = lax.ppermute(key_value, AXIS, forward)
    window = jnp.concatenate([passed, key_value], axis=1).reshape(2, 2 * SEQ, own, HEAD_DIM)
    allowed = (
        jnp.arange(2 * SEQ, dtype=jnp.int32)[None, :] <= slot[:, None] + SEQ
    ) & (key_ids[None, :] == own_ids[:, None])

    def masked_scores():
        scores = (
            jnp.einsum("qhd,khd->hqk", queries, window[0], preferred_element_type=FL) * score_scale
        )
        return jnp.where(allowed[None], scores, MASKED)

    scores = masked_scores()
    top_score = jnp.max(scores, axis=-1, keepdims=True)
    log_total = top_score + jnp.log(
        jnp.sum(jnp.exp(scores - top_score), axis=-1, keepdims=True)
    )
    probs = jnp.exp(scores - log_total).astype(BF)
    attended = jnp.einsum("hqk,khd->qhd", probs, window[1], preferred_element_type=FL)
    attended = attended.reshape(SEQ, span).astype(BF)
    w_shared, attended = lax.optimization_barrier((w_shared, attended))
    wide_s = -(-(hid_s + 1) // 128) * 128
    wide_e = -(-hid_e // 128) * 128
    full = wide_s + wide_e

    def columns(value, wide):
        return jnp.pad(value, ((0, 0), (0, wide - value.shape[1])))

    gate_side = jnp.concatenate([w_shared[:, :hid_s], gate.reshape(width, 1).astype(BF)], axis=1)
    w1 = jnp.concatenate(
        [
            columns(gate_side, wide_s),
            columns(expert_in[0][:, :hid_e], wide_e),
            columns(w_shared[:, hid_s:], wide_s),
            columns(expert_in[0][:, hid_e:], wide_e),
        ],
        axis=1,
    )
    w2 = jnp.concatenate(
        [
            jnp.pad(shared_out, ((0, wide_s - hid_s), (0, 0))),
            jnp.pad(expert_out[0], ((0, wide_e - hid_e), (0, 0))),
        ],
        axis=0,
    )
    hidden = inputs + team_scatter(dot(attended, w_out).astype(BF), 1).astype(FL)
    scale_mid = lax.rsqrt(jnp.mean(hidden * hidden, axis=-1, keepdims=True) + EPSILON)
    mid = (hidden * scale_mid * gain_mid).astype(BF)

    if layered:
        mid_all = gather(mid, teams, 2)
    else:
        mid_all = lax.all_gather(mid, AXIS, axis=0, tiled=True)
    mid_part, out_part, act_low, d_pre = feed(
        mid_all, grad_all, expert_weight[:, None], w1, w2, hid_s, wide_s
    )
    if layered:
        summed_mid, summed_out = scatter([mid_part, out_part], teams, 3)
    else:
        summed_mid = lax.psum_scatter(mid_part, AXIS, scatter_dimension=0, tiled=True)
        summed_out = lax.psum_scatter(out_part, AXIS, scatter_dimension=0, tiled=True)
    d_w1 = dot(mid_all, d_pre, ((0,), (0,)))
    d_w2 = dot(act_low, grad_all, ((0,), (0,)))
    shared_out_grad = d_w2[:hid_s]
    expert_out_grad = d_w2[wide_s : wide_s + hid_e]
    expert_in_grad = jnp.concatenate(
        [d_w1[:, wide_s : wide_s + hid_e], d_w1[:, full + wide_s : full + wide_s + hid_e]], axis=1
    )
    d_shared = jnp.concatenate([d_w1[:, :hid_s], d_w1[:, full : full + hid_s]], axis=1)
    gate_grad = d_w1[:, hid_s]
    shared_back = lax.all_to_all(
        d_shared.astype(BF).reshape(count, share, 2 * hid_s),
        AXIS,
        split_axis=0,
        concat_axis=0,
        tiled=True,
    )
    output = (hidden + summed_out.astype(FL)).astype(BF)

    grad_out = cotangent.astype(FL)
    d_mid = summed_mid.astype(FL)

    def norm_back(value, scale, gain, grad):
        unit = value * scale
        weighted = grad * gain
        inner = jnp.mean(weighted * unit, axis=-1, keepdims=True)
        return scale * (weighted - unit * inner), jnp.sum(grad * unit, axis=0)

    d_hidden_part, gain_mid_grad = norm_back(hidden, scale_mid, gain_mid, d_mid)
    d_hidden = grad_out + d_hidden_part
    d_attn = team_gather(d_hidden.astype(BF), 4)
    d_attended = dot(d_attn, w_out, ((1,), (1,))).astype(BF)
    out_grad = dot(attended, d_attn, ((0,), (0,))).astype(BF)
    out_part_grad = lax.psum_scatter(
        out_grad, AXIS, scatter_dimension=0, tiled=True, axis_index_groups=across
    )
    out_weight_grad = lax.ppermute(
        out_part_grad, AXIS, [(target, source) for source, target in deal]
    ).astype(FL)
    d_attended = d_attended.reshape(SEQ, own, HEAD_DIM)
    attention = jnp.exp(masked_scores() - log_total)
    d_attention = jnp.einsum("qhd,khd->hqk", d_attended, window[1], preferred_element_type=FL)
    row_delta = jnp.sum(attention * d_attention, axis=-1, keepdims=True)
    d_scores = (attention * (d_attention - row_delta)).astype(BF)
    d_queries = (
        jnp.einsum("hqk,khd->qhd", d_scores, window[0], preferred_element_type=FL) * score_scale
    )
    d_keys = jnp.einsum("hqk,qhd->khd", d_scores, queries, preferred_element_type=FL) * score_scale
    d_values = jnp.einsum(
        "hqk,qhd->khd", attention.astype(BF), d_attended, preferred_element_type=FL
    )
    d_kv = jnp.stack([d_keys.reshape(2 * SEQ, span), d_values.reshape(2 * SEQ, span)])
    returned = lax.ppermute(d_kv[:, :SEQ].astype(BF), AXIS, backward).astype(FL)
    d_kv = d_kv[:, SEQ:] + returned
    d_projected = jnp.concatenate(
        [
            unrotate(d_queries, cosine, sine).reshape(SEQ, span),
            unrotate(d_kv[0].reshape(SEQ, own, HEAD_DIM), cosine, sine).reshape(SEQ, span),
            d_kv[1],
        ],
        axis=1,
    ).astype(BF)
    d_projected, out_weight_grad = lax.optimization_barrier((d_projected, out_weight_grad))
    d_normed = team_scatter(dot(d_projected, w_qkv, ((1,), (1,))).astype(BF), 5).astype(FL)
    shared_in_grad = (
        shared_back.reshape(count, share, 2, hid_s)
        .transpose(1, 2, 0, 3)
        .reshape(share, -1)
        .astype(FL)
    )
    d_inputs, gain_in_grad = norm_back(inputs, scale_in, gain_in, d_normed)
    input_grad = d_hidden + d_inputs
    qkv_grad = dot(normed, d_projected, ((0,), (0,)))
    bias_grad = jnp.sum(d_projected.astype(FL), axis=0).reshape(3, own, HEAD_DIM)

    qkv_part = lax.psum_scatter(
        qkv_grad.astype(BF), AXIS, scatter_dimension=0, tiled=True, axis_index_groups=across
    )
    qkv_part = lax.all_to_all(
        qkv_part.reshape(team, share, 3 * span),
        AXIS,
        split_axis=0,
        concat_axis=0,
        tiled=True,
        axis_index_groups=in_team,
    )
    qkv_weight_grad = (
        qkv_part.reshape(team, share, 3, span)
        .transpose(1, 2, 0, 3)
        .reshape(share, 3 * width)
        .astype(FL)
    )
    bias_spread = lax.dynamic_update_slice_in_dim(
        jnp.zeros((3, heads, HEAD_DIM), FL), bias_grad, seat * own, 1
    )
    small_grads = jnp.concatenate(
        [
            gain_in_grad.reshape(count, share),
            bias_spread.reshape(count, bias_share),
            gain_mid_grad.reshape(count, share),
            gate_grad.reshape(count, share),
        ],
        axis=1,
    )
    if layered:
        entries = small_grads.shape[1]
        lanes = -(-entries // 2048) * 128
        small_grads = jnp.pad(small_grads, ((0, 0), (0, 16 * lanes - entries)))
        small_sum = scatter([small_grads.reshape(count * 16, lanes)], teams, 7)[0]
        small_sum = small_sum.reshape(-1)[:entries]
    else:
        small_sum = lax.psum_scatter(small_grads, AXIS, scatter_dimension=0, tiled=True)[0]
    return (
        output,
        input_grad,
        small_sum[:share],
        qkv_weight_grad,
        small_sum[share : share + bias_share],
        out_weight_grad,
        small_sum[share + bias_share : 2 * share + bias_share],
        small_sum[2 * share + bias_share :],
        shared_in_grad,
        shared_out_grad,
        expert_in_grad[None],
        expert_out_grad[None],
    )


def solution(mesh):
    row, flat, deep = P("fsdp", None), P("fsdp"), P("fsdp", None, None)
    return jax.shard_map(
        per_device,
        mesh=mesh,
        in_specs=(
            row, row, flat, row, row, row, flat, row, flat, row, flat, flat, row, row, deep, deep,
        ),
        out_specs=(row, row, flat, row, flat, row, flat, flat, row, row, deep, deep),
        check_vma=False,
    )
```

```python
import functools

import jax
import jax.numpy as jnp
from jax import lax
from jax.experimental import pallas as pl
from jax.experimental.pallas import tpu as pltpu
from jax.sharding import PartitionSpec as P

HEAD_DIM = 128
EXP_PARTS = 4
SEQ = 1024

EPSILON = 1e-06
THETA = 1000000.0
MASKED = -1e30
BF = jnp.bfloat16
FL = jnp.float32
AXIS = "fsdp"
MESH = pl.DeviceIdType.MESH


def place(length):
    me = lax.axis_index(AXIS)
    z, y, x, c = me // 8, (me // 4) % 2, (me // 2) % 2, me % 2

    def device(dz=0, y=y, x=x, c=c):
        return (((z + dz) * 2 + y) * 2 + x) * 2 + c

    return (z if length > 1 else z * 0), y, x, c, device


def greet(length, p, device, y, x, c):
    barrier = pltpu.get_barrier_semaphore()
    for other in (device(c=1 - c), device(x=1 - x), device(y=1 - y)):
        pl.semaphore_signal(barrier, inc=1, device_id=(other,), device_id_type=MESH)
    sides = ((-1, p > 0), (1, p < length - 1)) if length > 1 else ()
    for dz, there in sides:
        @pl.when(there)
        def _():
            pl.semaphore_signal(barrier, inc=1, device_id=(device(dz),), device_id_type=MESH)
    peers = 3
    for _, there in sides:
        peers = peers + there.astype(jnp.int32)
    pl.semaphore_wait(barrier, peers)


def line_order(p):
    return [
        p,
        jnp.where(p == 0, 1, p - 1),
        jnp.where(p == 0, 2, jnp.where(p == 3, 1, p + 1)),
        jnp.where(p < 2, 3, 0),
    ]


def gather_body(length, x_ref, o_ref, send_sem, recv_sem, own_sem, line=None):
    p, y, x, c, device = place(length)
    if line is None:
        greet(length, p, device, y, x, c)
        line = [lambda: None] * 5

    def block(h, z, yy, xx, cc):
        return o_ref.at[z, yy, xx, cc, h]

    def code(h, z, yy, xx, cc):
        return h * (8 * length) + ((z * 2 + yy) * 2 + xx) * 2 + cc

    def copy(src, h, where, slot, target):
        return pltpu.make_async_remote_copy(
            src_ref=src,
            dst_ref=block(h, *where),
            send_sem=send_sem.at[slot],
            recv_sem=recv_sem.at[code(h, *where)],
            device_id=(target,),
            device_id_type=MESH,
        )

    def arrived(h, where):
        copy(block(h, *where), h, where, 0, device(c=1 - c)).wait_recv()

    per_half = 9 * length
    started = []

    def send(src, h, where, slot, target, there=None):
        made = copy(src, h, where, h * per_half + slot, target)
        if there is None:
            made.start()
        else:
            pl.when(there)(made.start)
        started.append((made, there))

    own = [pltpu.make_async_copy(x_ref.at[h], block(h, p, y, x, c), own_sem.at[h]) for h in range(2)]
    for h in range(2):
        own[h].start()

    if length == 4:
        order = line_order(p)
    else:
        order = [p]

    def sides(h, z):
        first = (z, 1 - y, x, c) if h == 0 else (z, y, 1 - x, c)
        seconds = (
            [(z, y, 1 - x, c), (z, 1 - y, 1 - x, c)]
            if h == 0
            else [(z, 1 - y, x, c), (z, 1 - y, 1 - x, c)]
        )
        first_to = device(y=1 - y) if h == 0 else device(x=1 - x)
        second_to = device(x=1 - x) if h == 0 else device(y=1 - y)
        return first, seconds, first_to, second_to

    def stage_z(j):
        z = order[j]
        for h in range(2):
            where = (z, y, x, c)
            if j:
                arrived(h, where)
            src = block(h, *where) if j else x_ref.at[h]
            if length > 1:
                right = (p < length - 1) & (z <= p)
                left = (p > 0) & (z >= p)
                send(src, h, where, 9 * j, device(1), right)
                send(src, h, where, 9 * j + 1, device(-1), left)
            _, _, first_to, second_to = sides(h, z)
            send(src, h, where, 9 * j + 2, first_to)
            send(src, h, where, 9 * j + 3, second_to)
            send(src, h, where, 9 * j + 4, device(c=1 - c))

    def stage_first(j):
        z = order[j]
        for h in range(2):
            first, _, _, second_to = sides(h, z)
            arrived(h, first)
            send(block(h, *first), h, first, 9 * j + 5, second_to)
            send(block(h, *first), h, first, 9 * j + 6, device(c=1 - c))

    def stage_second(j):
        z = order[j]
        for i in range(2):
            for h in range(2):
                _, seconds, _, _ = sides(h, z)
                arrived(h, seconds[i])
                send(block(h, *seconds[i]), h, seconds[i], 9 * j + 7 + i, device(c=1 - c))

    line[0]()
    stage_z(0)
    for j in range(length):
        if j + 1 < length:
            stage_z(j + 1)
        stage_first(j)
        if j:
            stage_second(j - 1)
    stage_second(length - 1)
    line[1]()
    for j in range(length):
        for h in range(2):
            for yy, xx in ((y, x), (1 - y, x), (y, 1 - x), (1 - y, 1 - x)):
                arrived(h, (order[j], yy, xx, 1 - c))
    for h in range(2):
        own[h].wait()
    for step in line[2:]:
        step()
    for made, there in started:
        if there is None:
            made.wait_send()
        else:
            pl.when(there)(made.wait_send)


def gather(value, length, collective_id):
    rows, width = value.shape
    half = rows // 2
    out = pl.pallas_call(
        functools.partial(gather_body, length),
        out_shape=jax.ShapeDtypeStruct((length, 2, 2, 2, 2, half, width), value.dtype),
        in_specs=[pl.BlockSpec(memory_space=pltpu.VMEM)],
        out_specs=pl.BlockSpec(memory_space=pl.ANY),
        scratch_shapes=[
            pltpu.SemaphoreType.DMA((18 * length,)),
            pltpu.SemaphoreType.DMA((16 * length,)),
            pltpu.SemaphoreType.DMA((2,)),
        ],
        compiler_params=pltpu.CompilerParams(collective_id=collective_id, has_side_effects=True),
    )(value.reshape(2, half, width))
    return out.reshape(8 * length * rows, width)


def layer_and_line_body(many, *refs):
    x_ref, ins = refs[0], refs[1 : 1 + many]
    o_ref, outs = refs[1 + many], refs[2 + many : 2 + 2 * many]
    send_sem, recv_sem, own_sem, line_send, line_recv, line_own = refs[2 + 2 * many :]
    p, y, x, c, device = place(4)
    greet(4, p, device, y, x, c)
    order = line_order(p)
    started = []
    own = [pltpu.make_async_copy(ins[k], outs[k].at[p], line_own.at[k]) for k in range(many)]

    def copy(k, j, z, side):
        return pltpu.make_async_remote_copy(
            src_ref=outs[k].at[z] if j else ins[k],
            dst_ref=outs[k].at[z],
            send_sem=line_send.at[(k * 4 + j) * 2 + side],
            recv_sem=line_recv.at[k * 4 + z],
            device_id=(device(1 - 2 * side),),
            device_id_type=MESH,
        )

    def stage(j):
        z = order[j]
        for k in range(many):
            if j:
                pltpu.make_async_remote_copy(
                    src_ref=outs[k].at[z], dst_ref=outs[k].at[z], send_sem=line_send.at[0],
                    recv_sem=line_recv.at[k * 4 + z], device_id=(device(c=1 - c),),
                    device_id_type=MESH,
                ).wait_recv()
            else:
                own[k].start()
            for side, there in ((0, (p < 3) & (z <= p)), (1, (p > 0) & (z >= p))):
                made = copy(k, j, z, side)
                pl.when(there)(made.start)
                started.append((made, there))

    def finish():
        for k in range(many):
            own[k].wait()
        for made, there in started:
            pl.when(there)(made.wait_send)

    line = [functools.partial(stage, j) for j in range(4)] + [finish]
    gather_body(1, x_ref, o_ref, send_sem, recv_sem, own_sem, line)


def layer_and_line(value, others, collective_id):
    rows, width = value.shape
    half = rows // 2
    many = len(others)
    outs = pl.pallas_call(
        functools.partial(layer_and_line_body, many),
        out_shape=[jax.ShapeDtypeStruct((1, 2, 2, 2, 2, half, width), value.dtype)]
        + [jax.ShapeDtypeStruct((4,) + other.shape, other.dtype) for other in others],
        in_specs=[pl.BlockSpec(memory_space=pltpu.VMEM)] * (1 + many),
        out_specs=[pl.BlockSpec(memory_space=pl.ANY)] * (1 + many),
        scratch_shapes=[
            pltpu.SemaphoreType.DMA((18,)),
            pltpu.SemaphoreType.DMA((16,)),
            pltpu.SemaphoreType.DMA((2,)),
            pltpu.SemaphoreType.DMA((8 * many,)),
            pltpu.SemaphoreType.DMA((4 * many,)),
            pltpu.SemaphoreType.DMA((many,)),
        ],
        compiler_params=pltpu.CompilerParams(collective_id=collective_id, has_side_effects=True),
    )(value.reshape(2, half, width), *others)
    return [outs[0].reshape(8 * rows, width)] + [
        out.reshape((-1,) + out.shape[2:]) for out in outs[1:]
    ]


def sum_order(p):
    return [
        jnp.where(p < 2, 3, 0),
        jnp.where(p == 0, 2, jnp.where(p == 1, 0, jnp.where(p == 2, 3, 1))),
        jnp.where((p == 0) | (p == 2), 1, 2),
        p,
    ]


def add_rows(target, sources):
    rows_in_all = target.shape[0]
    row_step = min(16, rows_in_all)

    def body(i, _):
        rows = pl.ds(pl.multiple_of(i * row_step, row_step), row_step)
        value = sources[0][rows, :].astype(FL)
        for source in sources[1:]:
            value = value + source[rows, :].astype(FL)
        target[rows, :] = value.astype(target.dtype)
        return 0

    lax.fori_loop(0, rows_in_all // row_step, body, 0)


def line_sums(p, device, c, ins, outs, nears, arrivals, load_sem, send_sem, z_sem):
    many = len(ins)
    started = []

    def load(k, t):
        return pltpu.make_async_copy(ins[k].at[t], nears[k].at[t], load_sem.at[k * 4 + t])

    def begin():
        for t in range(4):
            for k in range(many):
                load(k, t).start()

    def step(t):
        for k in range(many):
            near = nears[k].at[t]
            load(k, t).wait()
            for side, there in ((0, (p > 0) & (p <= t)), (1, (p < 3) & (p >= t))):
                kept = jnp.where(p == t, 4, t) if side else t

                @pl.when(there)
                def _():
                    pltpu.make_async_remote_copy(
                        src_ref=near, dst_ref=arrivals[k].at[kept], send_sem=send_sem.at[0],
                        recv_sem=z_sem.at[(k * 4 + t) * 2 + side],
                        device_id=(device(c=1 - c),), device_id_type=MESH,
                    ).wait_recv()
                    add_rows(near, [near, arrivals[k].at[kept]])
            @pl.when(p == t)
            def _():
                add_rows(outs[k], [near])
            for side, there in ((0, p < t), (1, p > t)):
                kept = jnp.where(p - 1 == t, 4, t) if side else t
                slot = (k * 4 + t) * 2 + side
                made = pltpu.make_async_remote_copy(
                    src_ref=near, dst_ref=arrivals[k].at[kept], send_sem=send_sem.at[slot],
                    recv_sem=z_sem.at[slot],
                    device_id=(device(1 - 2 * side),), device_id_type=MESH,
                )
                pl.when(there)(made.start)
                started.append((made, there))

    def finish():
        for made, there in started:
            pl.when(there)(made.wait_send)

    return [begin] + [functools.partial(step, t) for t in sum_order(p)] + [finish]


def scatter_body(length, many, extra, *refs):
    in_refs, extra_in, refs = refs[:many], refs[many : many + extra], refs[many + extra :]
    o_refs, extra_out, refs = refs[:many], refs[many : many + extra], refs[many + extra :]
    (pair_in, near, first_in, second_in, z_in, total,
     send_sem, pair_sem, load_sem, first_sem, second_sem, z_sem) = refs[:12]
    if extra:
        p, y, x, c, device = place(4)
        greet(4, p, device, y, x, c)
        work = line_sums(
            p, device, c, extra_in, extra_out, refs[12 : 12 + extra],
            refs[12 + extra : 12 + 2 * extra], *refs[12 + 2 * extra :]
        )
        p = p * 0
    else:
        p, y, x, c, device = place(length)
        greet(length, p, device, y, x, c)
        work = []
    half, width = total.shape
    order = sum_order(p) if length == 4 else [0]
    places = range(length)
    started = []

    def part(g, z, far, cc):
        if g % 2 == 0:
            return in_refs[g // 2].at[z, :, (1 - x if far else x), cc, 0]
        return in_refs[g // 2].at[z, (1 - y if far else y), :, cc, 1]

    def send(src, dst, slot, sem, target, there=None):
        made = pltpu.make_async_remote_copy(
            src_ref=src, dst_ref=dst, send_sem=send_sem.at[slot], recv_sem=sem,
            device_id=(target,), device_id_type=MESH,
        )
        if there is None:
            made.start()
        else:
            pl.when(there)(made.start)
        started.append((made, there))
        return made

    first_to = (device(x=1 - x), device(y=1 - y))
    second_to = (device(y=1 - y), device(x=1 - x))
    place_s = (y, x)
    slot = lambda g, z, k: (g * length + z) * 6 + k
    pairs, loads, firsts, seconds = {}, {}, {}, {}
    for begin in work[:2]:
        begin()
    steps = [(q, n) for q in range(many) for n in places]
    for q in range(many):
        for far in (1, 0):
            for n in places:
                z = order[n]
                for g in (2 * q, 2 * q + 1):
                    k = (g * length + z) * 2 + far
                    pairs[g, n, far] = send(
                        part(g, z, far, 1 - c), pair_in.at[g, z, far], slot(g, z, far),
                        pair_sem.at[k], device(c=1 - c),
                    )
                    loads[g, n, far] = pltpu.make_async_copy(
                        part(g, z, far, c), near.at[g, z, far], load_sem.at[k]
                    )
                    loads[g, n, far].start()

    def stage_first(q, n):
        z = order[n]
        for g in (2 * q, 2 * q + 1):
            pairs[g, n, 1].wait_recv()
            loads[g, n, 1].wait()
            for s in range(2):
                add_rows(near.at[g, z, 1, s], [near.at[g, z, 1, s], pair_in.at[g, z, 1, s]])
            firsts[g, n] = send(
                near.at[g, z, 1], first_in.at[g, z], slot(g, z, 2),
                first_sem.at[g * length + z], first_to[g % 2],
            )

    def stage_second(q, n):
        z = order[n]
        for g in (2 * q, 2 * q + 1):
            s = 1 - place_s[g % 2]
            pairs[g, n, 0].wait_recv()
            loads[g, n, 0].wait()
            firsts[g, n].wait_recv()
            add_rows(near.at[g, z, 0, s],
                [near.at[g, z, 0, s], pair_in.at[g, z, 0, s], first_in.at[g, z, s]])
            seconds[g, n] = send(
                near.at[g, z, 0, s], second_in.at[g, z], slot(g, z, 3),
                second_sem.at[g * length + z], second_to[g % 2],
            )

    def stage_z(q, n):
        z = order[n]
        for g in (2 * q, 2 * q + 1):
            s = place_s[g % 2]
            o_half = o_refs[q].at[g % 2]
            seconds[g, n].wait_recv()
            sources = [near.at[g, z, 0, s], pair_in.at[g, z, 0, s], first_in.at[g, z, s],
                       second_in.at[g, z]]
            if length == 1:
                add_rows(o_half, sources)
                continue
            add_rows(total, sources)
            for side, sender in ((0, (p > 0) & (p <= z)), (1, (p < length - 1) & (p >= z))):
                @pl.when(sender)
                def _():
                    k = (g * length + z) * 2 + side
                    pltpu.make_async_remote_copy(
                        src_ref=near.at[g, z, 0, s], dst_ref=z_in.at[g, z, side],
                        send_sem=send_sem.at[0], recv_sem=z_sem.at[k],
                        device_id=(device(c=1 - c),), device_id_type=MESH,
                    ).wait_recv()
                    add_rows(total, [total, z_in.at[g, z, side]])
            @pl.when(p == z)
            def _():
                add_rows(o_half, [total])
            @pl.when(p != z)
            def _():
                add_rows(near.at[g, z, 0, s], [total])
            send(near.at[g, z, 0, s], z_in.at[g, z, 0], slot(g, z, 4),
                 z_sem.at[(g * length + z) * 2], device(1), p < z)
            send(near.at[g, z, 0, s], z_in.at[g, z, 1], slot(g, z, 5),
                 z_sem.at[(g * length + z) * 2 + 1], device(-1), p > z)

    count = len(steps)
    for i in range(count + 3):
        for stage, j in ((stage_first, i), (stage_z, i - 3), (stage_second, i - 1)):
            if 0 <= j < count:
                stage(*steps[j])
                if stage is stage_first and work:
                    work[2]()
    for step in work[3:]:
        step()
    for made, there in started:
        if there is None:
            made.wait_send()
        else:
            pl.when(there)(made.wait_send)


def scatter(values, length, collective_id, others=()):
    many, extra = len(values), len(others)
    rows, width = values[0].shape[0] // (8 * length), values[0].shape[1]
    half = rows // 2
    kind = values[0].dtype
    lanes = 2 * many
    others = [other.reshape((4, other.shape[0] // 4) + other.shape[1:]) for other in others]
    extra_scratch = []
    if extra:
        extra_scratch = (
            [pltpu.VMEM(other.shape, other.dtype) for other in others]
            + [pltpu.VMEM((5,) + other.shape[1:], other.dtype) for other in others]
            + [pltpu.SemaphoreType.DMA((n * extra,)) for n in (4, 8, 8)]
        )
    outs = pl.pallas_call(
        functools.partial(scatter_body, length, many, extra),
        out_shape=[jax.ShapeDtypeStruct((2, half, width), FL)] * many
        + [jax.ShapeDtypeStruct(other.shape[1:], other.dtype) for other in others],
        in_specs=[pl.BlockSpec(memory_space=pl.ANY)] * (many + extra),
        out_specs=[pl.BlockSpec(memory_space=pltpu.VMEM)] * (many + extra),
        scratch_shapes=[
            pltpu.VMEM((lanes, length, 2, 2, half, width), kind),
            pltpu.VMEM((lanes, length, 2, 2, half, width), kind),
            pltpu.VMEM((lanes, length, 2, half, width), kind),
            pltpu.VMEM((lanes, length, half, width), kind),
            pltpu.VMEM((lanes, length, 2, half, width), kind),
            pltpu.VMEM((half, width), FL),
            pltpu.SemaphoreType.DMA((6 * lanes * length,)),
            pltpu.SemaphoreType.DMA((2 * lanes * length,)),
            pltpu.SemaphoreType.DMA((2 * lanes * length,)),
            pltpu.SemaphoreType.DMA((lanes * length,)),
            pltpu.SemaphoreType.DMA((lanes * length,)),
            pltpu.SemaphoreType.DMA((2 * lanes * length,)),
        ] + extra_scratch,
        compiler_params=pltpu.CompilerParams(
            collective_id=collective_id, has_side_effects=True, vmem_limit_bytes=62 << 20
        ),
    )(*[value.reshape(length, 2, 2, 2, 2, half, width) for value in values], *others)
    return [out.reshape(rows, width) for out in outs[:many]] + list(outs[many:])


def side_by_side(value, parts):
    blocks, rows, columns = value.shape
    columns = columns // parts

    def body(in_ref, out_ref):
        for part in range(parts):
            pieces = [
                in_ref[block].astype(FL)[:, part * columns : (part + 1) * columns]
                for block in range(blocks)
            ]
            lanes = pl.ds(part * blocks * columns, blocks * columns)
            out_ref[:, lanes] = jnp.concatenate(pieces, axis=1)

    return pl.pallas_call(
        body, out_shape=jax.ShapeDtypeStruct((rows, parts * blocks * columns), FL)
    )(value)


def dot(a, b, dims=((1,), (0,))):
    return lax.dot_general(a, b, (dims, ((), ())), preferred_element_type=FL)


def feed_body(mid_ref, grad_ref, weight_ref, w1_ref, w2_ref, part_ref, out_ref, act_ref, pre_ref,
              *, gate_column, shared_width):
    full = w2_ref.shape[0]
    mid, grad = mid_ref[...], grad_ref[...]
    pre = dot(mid, w1_ref[...])
    grad_act = dot(grad, w2_ref[...], ((1,), (1,)))
    gate_pre, up = pre[:, :full], pre[:, full:]
    shared_scale = jax.nn.sigmoid(gate_pre[:, gate_column : gate_column + 1])
    column = lax.broadcasted_iota(jnp.int32, gate_pre.shape, 1)
    factor = jnp.where(column < shared_width, shared_scale, weight_ref[...])
    sig = jax.nn.sigmoid(gate_pre)
    silu = gate_pre * sig
    act = silu * up
    low = (act * factor).astype(BF)
    logit = jnp.sum(
        act[:, :shared_width] * grad_act[:, :shared_width], axis=1, keepdims=True
    )
    d_logit = logit * shared_scale * (1.0 - shared_scale)
    scaled = grad_act * factor
    d_gate = scaled * up * sig * (1.0 + gate_pre * (1.0 - sig))
    d_gate = jnp.where(column == gate_column, d_logit, d_gate)
    act_ref[...] = low
    pre_ref[:, :full] = d_gate.astype(BF)
    pre_ref[:, full:] = (scaled * silu).astype(BF)
    part_ref[...] = dot(pre_ref[...], w1_ref[...], ((1,), (1,))).astype(BF)
    out_ref[...] = dot(low, w2_ref[...]).astype(BF)


def feed(mid, grad, weight, w1, w2, gate_column, shared_width):
    tokens, width = mid.shape
    full = w2.shape[0]
    block = 256
    row = lambda columns: pl.BlockSpec((block, columns), lambda i: (i, 0))
    whole = lambda shape: pl.BlockSpec(
        shape, lambda i: (0, 0), pipeline_mode=pl.Buffered(buffer_count=1)
    )
    return pl.pallas_call(
        functools.partial(feed_body, gate_column=gate_column, shared_width=shared_width),
        grid=(tokens // block,),
        out_shape=(
            jax.ShapeDtypeStruct((tokens, width), BF),
            jax.ShapeDtypeStruct((tokens, width), BF),
            jax.ShapeDtypeStruct((tokens, full), BF),
            jax.ShapeDtypeStruct((tokens, 2 * full), BF),
        ),
        in_specs=[row(width), row(width), row(1), whole(w1.shape), whole(w2.shape)],
        out_specs=(row(width), row(width), row(full), row(2 * full)),
        compiler_params=pltpu.CompilerParams(vmem_limit_bytes=56 << 20),
        cost_estimate=pl.CostEstimate(
            flops=12 * tokens * width * full, bytes_accessed=12 * tokens * width,
            transcendentals=tokens * full,
        ),
    )(mid, grad, weight, w1, w2)


def rms_norm(vector, factor):
    return vector * lax.rsqrt(jnp.mean(vector * vector, axis=-1, keepdims=True) + EPSILON) * factor


def rotate(vector, cosine, sine):
    middle = vector.shape[-1] // 2
    turned = jnp.concatenate([-vector[..., middle:], vector[..., :middle]], axis=-1)
    return vector * cosine + turned * sine


def unrotate(grad, cosine, sine):
    middle = grad.shape[-1] // 2
    scaled = grad * sine
    turned = jnp.concatenate([scaled[..., middle:], -scaled[..., :middle]], axis=-1)
    return grad * cosine + turned


def pair_weight_table(expert_ids, route_weights, order_row, expert_count, capacity):
    rows, top = expert_ids.shape
    pairs = rows * top
    flat = expert_ids.reshape(pairs)
    index = jnp.arange(pairs, dtype=jnp.int32)
    turn = jnp.sum(
        jnp.where(order_row[None, :] == index[:, None], index[None, :], 0), axis=1, dtype=jnp.int32
    )
    before = (turn[None, :] < turn[:, None]) & (flat[None, :] == flat[:, None])
    slots = jnp.sum(before.astype(jnp.int32), axis=1, dtype=jnp.int32)
    kept = (slots < capacity).astype(FL).reshape(rows, top)
    hit = expert_ids[:, :, None] == jnp.arange(expert_count, dtype=jnp.int32)[None, None, :]
    return jnp.sum(jnp.where(hit, (route_weights * kept)[:, :, None], 0.0), axis=1)


def per_device(
    tokens,
    cotangent,
    segment_ids,
    expert_ids,
    route_weights,
    pair_order,
    norm_in_gain,
    qkv_weight,
    qkv_bias,
    out_weight,
    norm_mid_gain,
    shared_gate,
    shared_in,
    shared_out,
    expert_in,
    expert_out,
):
    rows, width = tokens.shape
    count = lax.axis_size(AXIS)
    me = lax.axis_index(AXIS)
    team = SEQ // rows
    teams = count // team
    slab = me // team
    seat = me % team
    heads = width // HEAD_DIM
    own = heads // team
    span = own * HEAD_DIM
    top = expert_ids.shape[1]
    expert_count = count // EXP_PARTS
    capacity = (9 * rows * top + 8 * expert_count - 1) // (8 * expert_count)
    score_scale = HEAD_DIM ** (-0.5)
    in_team = [[s * team + p for p in range(team)] for s in range(teams)]
    across = [[s * team + p for s in range(teams)] for p in range(team)]
    share = width // count
    bias_share = 3 * width // count
    hid_s = shared_out.shape[0]
    hid_e = expert_out.shape[1]

    layered = team == 8 and teams == 4

    def team_gather(value, call):
        if layered:
            return gather(value, 1, call)
        return lax.all_gather(value, AXIS, axis=0, tiled=True, axis_index_groups=in_team)

    def team_scatter(value, call):
        if layered:
            return scatter([value], 1, call)[0]
        return lax.psum_scatter(
            value, AXIS, scatter_dimension=0, tiled=True, axis_index_groups=in_team
        )

    table = pair_weight_table(expert_ids, route_weights, pair_order[0], expert_count, capacity)
    packed = jnp.concatenate(
        [
            norm_in_gain.astype(FL),
            qkv_bias.astype(FL),
            norm_mid_gain.astype(FL),
            shared_gate.astype(FL),
            segment_ids.astype(FL),
            table.T.reshape(-1),
        ]
    )
    if layered:
        entries = packed.shape[0]
        lanes = -(-entries // 2048) * 128
        packed = jnp.pad(packed, (0, 16 * lanes - entries)).reshape(16, lanes)
        small = gather(packed, teams, 6).reshape(count, 16 * lanes)[:, :entries]
    else:
        small = lax.all_gather(packed[None], AXIS, axis=0, tiled=True)
    qkv_weight, small = lax.optimization_barrier((qkv_weight, small))
    edge = share
    gain_in = small[:, :edge].reshape(1, width)
    bias = small[:, edge : edge + bias_share].reshape(3, heads, HEAD_DIM)
    edge += bias_share
    gain_mid = small[:, edge : edge + share].reshape(1, width)
    edge += share
    gate = small[:, edge : edge + share].reshape(1, width)
    edge += share
    ids_all = small[:, edge : edge + rows]
    edge += rows
    tables = small[:, edge:].reshape(count, expert_count, rows)
    expert_weight = lax.dynamic_index_in_dim(tables, me // EXP_PARTS, 1, False).reshape(-1)

    mine = qkv_weight.reshape(share, 3, team, span).transpose(2, 0, 1, 3)
    mine = lax.all_to_all(
        mine.reshape(team, share, 3 * span),
        AXIS,
        split_axis=0,
        concat_axis=0,
        tiled=True,
        axis_index_groups=in_team,
    )
    deal = [(p * teams + s, s * team + p) for s in range(teams) for p in range(team)]
    mine = mine.reshape(team * share, 3 * span)
    out_rows = lax.ppermute(out_weight, AXIS, deal)
    inputs = tokens.astype(FL)
    scale_in = lax.rsqrt(jnp.mean(inputs * inputs, axis=-1, keepdims=True) + EPSILON)
    normed = (inputs * scale_in * gain_in).astype(BF)
    if layered:
        normed, w_qkv, w_out = layer_and_line(normed, [mine, out_rows], 0)
    else:
        normed = team_gather(normed, 0)
        w_qkv, w_out = [
            lax.all_gather(value, AXIS, axis=0, tiled=True, axis_index_groups=across)
            for value in (mine, out_rows)
        ]
    bias_own = lax.dynamic_slice_in_dim(bias, seat * own, own, 1).reshape(1, 3 * span)

    shared_in, normed = lax.optimization_barrier((shared_in, normed))

    shared_cols = shared_in.reshape(share, 2, count, hid_s).transpose(2, 0, 1, 3)
    w_shared = lax.all_to_all(
        shared_cols.reshape(count, share, 2 * hid_s),
        AXIS,
        split_axis=0,
        concat_axis=0,
        tiled=True,
    ).reshape(width, 2 * hid_s)
    grad_all = lax.all_gather(cotangent, AXIS, axis=0, tiled=True)

    own_ids = lax.dynamic_slice_in_dim(ids_all, slab * team, team, 0).reshape(SEQ)
    prev_ids = lax.dynamic_slice_in_dim(
        ids_all, jnp.maximum(slab - 1, 0) * team, team, 0
    ).reshape(SEQ)
    key_ids = jnp.concatenate([jnp.where(slab > 0, prev_ids, -1.0), own_ids])
    slot = jnp.arange(SEQ, dtype=jnp.int32)
    earlier = (key_ids[None, :] < own_ids[:, None]).astype(jnp.int32)
    positions = (SEQ + slot - jnp.sum(earlier, axis=1, dtype=jnp.int32)).astype(FL)
    inverse = THETA ** (-jnp.arange(0, HEAD_DIM, 2, dtype=FL) / HEAD_DIM)
    angles = positions[:, None] * inverse[None, :]
    angles = jnp.concatenate([angles, angles], axis=-1)
    cosine = jnp.cos(angles)[:, None, :]
    sine = jnp.sin(angles)[:, None, :]

    projected = dot(normed, w_qkv) + bias_own
    queries = rotate(projected[:, :span].reshape(SEQ, own, HEAD_DIM), cosine, sine).astype(BF)
    keys = rotate(projected[:, span : 2 * span].reshape(SEQ, own, HEAD_DIM), cosine, sine)
    key_value = jnp.stack([keys.astype(BF).reshape(SEQ, span), projected[:, 2 * span :].astype(BF)])
    forward = [(source, source + team) for source in range(count - team)]
    backward = [(target, source) for source, target in forward]
    passed = lax.ppermute(key_value, AXIS, forward)
    window = jnp.concatenate([passed, key_value], axis=1).reshape(2, 2 * SEQ, own, HEAD_DIM)
    allowed = (
        jnp.arange(2 * SEQ, dtype=jnp.int32)[None, :] <= slot[:, None] + SEQ
    ) & (key_ids[None, :] == own_ids[:, None])

    def masked_scores():
        scores = (
            jnp.einsum("qhd,khd->hqk", queries, window[0], preferred_element_type=FL) * score_scale
        )
        return jnp.where(allowed[None], scores, MASKED)

    scores = masked_scores()
    top_score = jnp.max(scores, axis=-1, keepdims=True)
    log_total = top_score + jnp.log(
        jnp.sum(jnp.exp(scores - top_score), axis=-1, keepdims=True)
    )
    probs = jnp.exp(scores - log_total).astype(BF)
    attended = jnp.einsum("hqk,khd->qhd", probs, window[1], preferred_element_type=FL)
    attended = attended.reshape(SEQ, span).astype(BF)
    w_shared, attended = lax.optimization_barrier((w_shared, attended))
    wide_s = -(-(hid_s + 1) // 128) * 128
    wide_e = -(-hid_e // 128) * 128
    full = wide_s + wide_e

    def columns(value, wide):
        return jnp.pad(value, ((0, 0), (0, wide - value.shape[1])))

    gate_side = jnp.concatenate([w_shared[:, :hid_s], gate.reshape(width, 1).astype(BF)], axis=1)
    w1 = jnp.concatenate(
        [
            columns(gate_side, wide_s),
            columns(expert_in[0][:, :hid_e], wide_e),
            columns(w_shared[:, hid_s:], wide_s),
            columns(expert_in[0][:, hid_e:], wide_e),
        ],
        axis=1,
    )
    w2 = jnp.concatenate(
        [
            jnp.pad(shared_out, ((0, wide_s - hid_s), (0, 0))),
            jnp.pad(expert_out[0], ((0, wide_e - hid_e), (0, 0))),
        ],
        axis=0,
    )
    hidden = inputs + team_scatter(dot(attended, w_out).astype(BF), 1).astype(FL)
    scale_mid = lax.rsqrt(jnp.mean(hidden * hidden, axis=-1, keepdims=True) + EPSILON)
    mid = (hidden * scale_mid * gain_mid).astype(BF)

    if layered:
        mid_all = gather(mid, teams, 2)
    else:
        mid_all = lax.all_gather(mid, AXIS, axis=0, tiled=True)
    mid_part, out_part, act_low, d_pre = feed(
        mid_all, grad_all, expert_weight[:, None], w1, w2, hid_s, wide_s
    )
    if layered:
        summed_mid, summed_out = scatter([mid_part, out_part], teams, 3)
    else:
        summed_mid = lax.psum_scatter(mid_part, AXIS, scatter_dimension=0, tiled=True)
        summed_out = lax.psum_scatter(out_part, AXIS, scatter_dimension=0, tiled=True)
    d_w1 = dot(mid_all, d_pre, ((0,), (0,)))
    d_w2 = dot(act_low, grad_all, ((0,), (0,)))
    expert_in_grad = jnp.concatenate(
        [d_w1[:, wide_s : wide_s + hid_e], d_w1[:, full + wide_s : full + wide_s + hid_e]], axis=1
    )
    d_shared = jnp.concatenate([d_w1[:, :hid_s], d_w1[:, full : full + hid_s]], axis=1)
    gate_grad = d_w1[:, hid_s]
    shared_back = lax.all_to_all(
        d_shared.astype(BF).reshape(count, share, 2 * hid_s),
        AXIS,
        split_axis=0,
        concat_axis=0,
        tiled=True,
    )
    output = (hidden + summed_out.astype(FL)).astype(BF)

    grad_out = cotangent.astype(FL)
    d_mid = summed_mid.astype(FL)

    def norm_back(value, scale, gain, grad):
        unit = value * scale
        weighted = grad * gain
        inner = jnp.mean(weighted * unit, axis=-1, keepdims=True)
        return scale * (weighted - unit * inner), jnp.sum(grad * unit, axis=0)

    d_hidden_part, gain_mid_grad = norm_back(hidden, scale_mid, gain_mid, d_mid)
    d_hidden = grad_out + d_hidden_part
    d_attn = team_gather(d_hidden.astype(BF), 4)
    d_attended = dot(d_attn, w_out, ((1,), (1,))).astype(BF)
    out_grad = dot(attended, d_attn, ((0,), (0,))).astype(BF)
    d_attended = d_attended.reshape(SEQ, own, HEAD_DIM)
    attention = jnp.exp(masked_scores() - log_total)
    d_attention = jnp.einsum("qhd,khd->hqk", d_attended, window[1], preferred_element_type=FL)
    row_delta = jnp.sum(attention * d_attention, axis=-1, keepdims=True)
    d_scores = (attention * (d_attention - row_delta)).astype(BF)
    d_queries = (
        jnp.einsum("hqk,khd->qhd", d_scores, window[0], preferred_element_type=FL) * score_scale
    )
    d_keys = jnp.einsum("hqk,qhd->khd", d_scores, queries, preferred_element_type=FL) * score_scale
    d_values = jnp.einsum(
        "hqk,qhd->khd", attention.astype(BF), d_attended, preferred_element_type=FL
    )
    d_kv = jnp.stack([d_keys.reshape(2 * SEQ, span), d_values.reshape(2 * SEQ, span)])
    returned = lax.ppermute(d_kv[:, :SEQ].astype(BF), AXIS, backward).astype(FL)
    d_kv = d_kv[:, SEQ:] + returned
    d_projected = jnp.concatenate(
        [
            unrotate(d_queries, cosine, sine).reshape(SEQ, span),
            unrotate(d_kv[0].reshape(SEQ, own, HEAD_DIM), cosine, sine).reshape(SEQ, span),
            d_kv[1],
        ],
        axis=1,
    ).astype(BF)
    d_projected, shared_back, d_w2 = lax.optimization_barrier((d_projected, shared_back, d_w2))
    d_normed = dot(d_projected, w_qkv, ((1,), (1,))).astype(BF)
    qkv_grad = dot(normed, d_projected, ((0,), (0,))).astype(BF)
    if layered:
        d_normed, qkv_part, out_part_grad = scatter([d_normed], 1, 5, [qkv_grad, out_grad])
    else:
        d_normed = team_scatter(d_normed, 5).astype(FL)
        qkv_part, out_part_grad = [
            lax.psum_scatter(
                value, AXIS, scatter_dimension=0, tiled=True, axis_index_groups=across
            )
            for value in (qkv_grad, out_grad)
        ]
    out_weight_grad = lax.ppermute(
        out_part_grad, AXIS, [(target, source) for source, target in deal]
    ).astype(FL)
    d_inputs, gain_in_grad = norm_back(inputs, scale_in, gain_in, d_normed)
    input_grad = d_hidden + d_inputs
    bias_grad = jnp.sum(d_projected.astype(FL), axis=0).reshape(3, own, HEAD_DIM)

    if layered:
        shared_in_grad = side_by_side(shared_back, 2)
    else:
        shared_in_grad = (
            shared_back.reshape(count, share, 2, hid_s)
            .transpose(1, 2, 0, 3)
            .reshape(share, -1)
            .astype(FL)
        )

    shared_out_grad = d_w2[:hid_s]
    expert_out_grad = d_w2[wide_s : wide_s + hid_e]
    qkv_part = lax.all_to_all(
        qkv_part.reshape(team, share, 3 * span),
        AXIS,
        split_axis=0,
        concat_axis=0,
        tiled=True,
        axis_index_groups=in_team,
    )
    qkv_weight_grad = (
        qkv_part.reshape(team, share, 3, span)
        .transpose(1, 2, 0, 3)
        .reshape(share, 3 * width)
        .astype(FL)
    )
    bias_spread = lax.dynamic_update_slice_in_dim(
        jnp.zeros((3, heads, HEAD_DIM), FL), bias_grad, seat * own, 1
    )
    small_grads = jnp.concatenate(
        [
            gain_in_grad.reshape(count, share),
            bias_spread.reshape(count, bias_share),
            gain_mid_grad.reshape(count, share),
            gate_grad.reshape(count, share),
        ],
        axis=1,
    )
    if layered:
        entries = small_grads.shape[1]
        lanes = -(-entries // 2048) * 128
        small_grads = jnp.pad(small_grads, ((0, 0), (0, 16 * lanes - entries)))
        small_sum = scatter([small_grads.reshape(count * 16, lanes)], teams, 7)[0]
        small_sum = small_sum.reshape(-1)[:entries]
    else:
        small_sum = lax.psum_scatter(small_grads, AXIS, scatter_dimension=0, tiled=True)[0]
    return (
        output,
        input_grad,
        small_sum[:share],
        qkv_weight_grad,
        small_sum[share : share + bias_share],
        out_weight_grad,
        small_sum[share + bias_share : 2 * share + bias_share],
        small_sum[2 * share + bias_share :],
        shared_in_grad,
        shared_out_grad,
        expert_in_grad[None],
        expert_out_grad[None],
    )


def solution(mesh):
    row, flat, deep = P("fsdp", None), P("fsdp"), P("fsdp", None, None)
    return jax.shard_map(
        per_device,
        mesh=mesh,
        in_specs=(
            row, row, flat, row, row, row, flat, row, flat, row, flat, flat, row, row, deep, deep,
        ),
        out_specs=(row, row, flat, row, flat, row, flat, flat, row, row, deep, deep),
        check_vma=False,
    )
```

```python
import functools

import jax
import jax.numpy as jnp
from jax import lax
from jax.experimental import pallas as pl
from jax.experimental.pallas import tpu as pltpu
from jax.sharding import PartitionSpec as P

HEAD_DIM = 128
EXP_PARTS = 4
SEQ = 1024

EPSILON = 1e-06
THETA = 1000000.0
MASKED = -1e30
BF = jnp.bfloat16
FL = jnp.float32
AXIS = "fsdp"
MESH = pl.DeviceIdType.MESH


def place(length):
    me = lax.axis_index(AXIS)
    z, y, x, c = me // 8, (me // 4) % 2, (me // 2) % 2, me % 2

    def device(dz=0, y=y, x=x, c=c):
        return (((z + dz) * 2 + y) * 2 + x) * 2 + c

    return (z if length > 1 else z * 0), y, x, c, device


def greet(length, p, device, y, x, c):
    barrier = pltpu.get_barrier_semaphore()
    for other in (device(c=1 - c), device(x=1 - x), device(y=1 - y)):
        pl.semaphore_signal(barrier, inc=1, device_id=(other,), device_id_type=MESH)
    sides = ((-1, p > 0), (1, p < length - 1)) if length > 1 else ()
    for dz, there in sides:
        @pl.when(there)
        def _():
            pl.semaphore_signal(barrier, inc=1, device_id=(device(dz),), device_id_type=MESH)
    peers = 3
    for _, there in sides:
        peers = peers + there.astype(jnp.int32)
    pl.semaphore_wait(barrier, peers)


def line_order(p):
    return [
        p,
        jnp.where(p == 0, 1, p - 1),
        jnp.where(p == 0, 2, jnp.where(p == 3, 1, p + 1)),
        jnp.where(p < 2, 3, 0),
    ]


def gather_body(length, x_ref, o_ref, send_sem, recv_sem, own_sem, line=None):
    p, y, x, c, device = place(length)
    if line is None:
        greet(length, p, device, y, x, c)
        line = [lambda: None] * 5

    def block(h, z, yy, xx, cc):
        return o_ref.at[z, yy, xx, cc, h]

    def code(h, z, yy, xx, cc):
        return h * (8 * length) + ((z * 2 + yy) * 2 + xx) * 2 + cc

    def copy(src, h, where, slot, target):
        return pltpu.make_async_remote_copy(
            src_ref=src,
            dst_ref=block(h, *where),
            send_sem=send_sem.at[slot],
            recv_sem=recv_sem.at[code(h, *where)],
            device_id=(target,),
            device_id_type=MESH,
        )

    def arrived(h, where):
        copy(block(h, *where), h, where, 0, device(c=1 - c)).wait_recv()

    per_half = 9 * length
    started = []

    def send(src, h, where, slot, target, there=None):
        made = copy(src, h, where, h * per_half + slot, target)
        if there is None:
            made.start()
        else:
            pl.when(there)(made.start)
        started.append((made, there))

    own = [pltpu.make_async_copy(x_ref.at[h], block(h, p, y, x, c), own_sem.at[h]) for h in range(2)]
    for h in range(2):
        own[h].start()

    if length == 4:
        order = line_order(p)
    else:
        order = [p]

    def sides(h, z):
        first = (z, 1 - y, x, c) if h == 0 else (z, y, 1 - x, c)
        seconds = (
            [(z, y, 1 - x, c), (z, 1 - y, 1 - x, c)]
            if h == 0
            else [(z, 1 - y, x, c), (z, 1 - y, 1 - x, c)]
        )
        first_to = device(y=1 - y) if h == 0 else device(x=1 - x)
        second_to = device(x=1 - x) if h == 0 else device(y=1 - y)
        return first, seconds, first_to, second_to

    def stage_z(j):
        z = order[j]
        for h in range(2):
            where = (z, y, x, c)
            if j:
                arrived(h, where)
            src = block(h, *where) if j else x_ref.at[h]
            if length > 1:
                right = (p < length - 1) & (z <= p)
                left = (p > 0) & (z >= p)
                send(src, h, where, 9 * j, device(1), right)
                send(src, h, where, 9 * j + 1, device(-1), left)
            _, _, first_to, second_to = sides(h, z)
            send(src, h, where, 9 * j + 2, first_to)
            send(src, h, where, 9 * j + 3, second_to)
            send(src, h, where, 9 * j + 4, device(c=1 - c))

    def stage_first(j):
        z = order[j]
        for h in range(2):
            first, _, _, second_to = sides(h, z)
            arrived(h, first)
            send(block(h, *first), h, first, 9 * j + 5, second_to)
            send(block(h, *first), h, first, 9 * j + 6, device(c=1 - c))

    def stage_second(j):
        z = order[j]
        for i in range(2):
            for h in range(2):
                _, seconds, _, _ = sides(h, z)
                arrived(h, seconds[i])
                send(block(h, *seconds[i]), h, seconds[i], 9 * j + 7 + i, device(c=1 - c))

    line[0]()
    stage_z(0)
    for j in range(length):
        if j + 1 < length:
            stage_z(j + 1)
        stage_first(j)
        if j:
            stage_second(j - 1)
    stage_second(length - 1)
    line[1]()
    for j in range(length):
        for h in range(2):
            for yy, xx in ((y, x), (1 - y, x), (y, 1 - x), (1 - y, 1 - x)):
                arrived(h, (order[j], yy, xx, 1 - c))
    for h in range(2):
        own[h].wait()
    for step in line[2:]:
        step()
    for made, there in started:
        if there is None:
            made.wait_send()
        else:
            pl.when(there)(made.wait_send)


def gather(value, length, collective_id):
    rows, width = value.shape
    half = rows // 2
    out = pl.pallas_call(
        functools.partial(gather_body, length),
        out_shape=jax.ShapeDtypeStruct((length, 2, 2, 2, 2, half, width), value.dtype),
        in_specs=[pl.BlockSpec(memory_space=pltpu.VMEM)],
        out_specs=pl.BlockSpec(memory_space=pl.ANY),
        scratch_shapes=[
            pltpu.SemaphoreType.DMA((18 * length,)),
            pltpu.SemaphoreType.DMA((16 * length,)),
            pltpu.SemaphoreType.DMA((2,)),
        ],
        compiler_params=pltpu.CompilerParams(collective_id=collective_id, has_side_effects=True),
    )(value.reshape(2, half, width))
    return out.reshape(8 * length * rows, width)


def layer_and_line_body(many, *refs):
    x_ref, ins = refs[0], refs[1 : 1 + many]
    o_ref, outs = refs[1 + many], refs[2 + many : 2 + 2 * many]
    send_sem, recv_sem, own_sem, line_send, line_recv, line_own = refs[2 + 2 * many :]
    p, y, x, c, device = place(4)
    greet(4, p, device, y, x, c)
    order = line_order(p)
    started = []
    own = [pltpu.make_async_copy(ins[k], outs[k].at[p], line_own.at[k]) for k in range(many)]

    def copy(k, j, z, side):
        return pltpu.make_async_remote_copy(
            src_ref=outs[k].at[z] if j else ins[k],
            dst_ref=outs[k].at[z],
            send_sem=line_send.at[(k * 4 + j) * 2 + side],
            recv_sem=line_recv.at[k * 4 + z],
            device_id=(device(1 - 2 * side),),
            device_id_type=MESH,
        )

    def stage(j):
        z = order[j]
        for k in range(many):
            if j:
                pltpu.make_async_remote_copy(
                    src_ref=outs[k].at[z], dst_ref=outs[k].at[z], send_sem=line_send.at[0],
                    recv_sem=line_recv.at[k * 4 + z], device_id=(device(c=1 - c),),
                    device_id_type=MESH,
                ).wait_recv()
            else:
                own[k].start()
            for side, there in ((0, (p < 3) & (z <= p)), (1, (p > 0) & (z >= p))):
                made = copy(k, j, z, side)
                pl.when(there)(made.start)
                started.append((made, there))

    def finish():
        for k in range(many):
            own[k].wait()
        for made, there in started:
            pl.when(there)(made.wait_send)

    line = [functools.partial(stage, j) for j in range(4)] + [finish]
    gather_body(1, x_ref, o_ref, send_sem, recv_sem, own_sem, line)


def layer_and_line(value, others, collective_id):
    rows, width = value.shape
    half = rows // 2
    many = len(others)
    outs = pl.pallas_call(
        functools.partial(layer_and_line_body, many),
        out_shape=[jax.ShapeDtypeStruct((1, 2, 2, 2, 2, half, width), value.dtype)]
        + [jax.ShapeDtypeStruct((4,) + other.shape, other.dtype) for other in others],
        in_specs=[pl.BlockSpec(memory_space=pltpu.VMEM)] * (1 + many),
        out_specs=[pl.BlockSpec(memory_space=pl.ANY)] * (1 + many),
        scratch_shapes=[
            pltpu.SemaphoreType.DMA((18,)),
            pltpu.SemaphoreType.DMA((16,)),
            pltpu.SemaphoreType.DMA((2,)),
            pltpu.SemaphoreType.DMA((8 * many,)),
            pltpu.SemaphoreType.DMA((4 * many,)),
            pltpu.SemaphoreType.DMA((many,)),
        ],
        compiler_params=pltpu.CompilerParams(collective_id=collective_id, has_side_effects=True),
    )(value.reshape(2, half, width), *others)
    return [outs[0].reshape(8 * rows, width)] + [
        out.reshape((-1,) + out.shape[2:]) for out in outs[1:]
    ]


def sum_order(p):
    return [
        jnp.where(p < 2, 3, 0),
        jnp.where(p == 0, 2, jnp.where(p == 1, 0, jnp.where(p == 2, 3, 1))),
        jnp.where((p == 0) | (p == 2), 1, 2),
        p,
    ]


def add_rows(target, sources):
    rows_in_all = target.shape[0]
    row_step = min(16, rows_in_all)

    def body(i, _):
        rows = pl.ds(pl.multiple_of(i * row_step, row_step), row_step)
        value = sources[0][rows, :].astype(FL)
        for source in sources[1:]:
            value = value + source[rows, :].astype(FL)
        target[rows, :] = value.astype(target.dtype)
        return 0

    lax.fori_loop(0, rows_in_all // row_step, body, 0)


def line_sums(p, device, c, ins, outs, nears, arrivals, load_sem, send_sem, z_sem):
    many = len(ins)
    started = []

    def load(k, t):
        return pltpu.make_async_copy(ins[k].at[t], nears[k].at[t], load_sem.at[k * 4 + t])

    def begin():
        for t in range(4):
            for k in range(many):
                load(k, t).start()

    def step(t):
        for k in range(many):
            near = nears[k].at[t]
            load(k, t).wait()
            for side, there in ((0, (p > 0) & (p <= t)), (1, (p < 3) & (p >= t))):
                kept = jnp.where(p == t, 4, t) if side else t

                @pl.when(there)
                def _():
                    pltpu.make_async_remote_copy(
                        src_ref=near, dst_ref=arrivals[k].at[kept], send_sem=send_sem.at[0],
                        recv_sem=z_sem.at[(k * 4 + t) * 2 + side],
                        device_id=(device(c=1 - c),), device_id_type=MESH,
                    ).wait_recv()
                    add_rows(near, [near, arrivals[k].at[kept]])
            @pl.when(p == t)
            def _():
                add_rows(outs[k], [near])
            for side, there in ((0, p < t), (1, p > t)):
                kept = jnp.where(p - 1 == t, 4, t) if side else t
                slot = (k * 4 + t) * 2 + side
                made = pltpu.make_async_remote_copy(
                    src_ref=near, dst_ref=arrivals[k].at[kept], send_sem=send_sem.at[slot],
                    recv_sem=z_sem.at[slot],
                    device_id=(device(1 - 2 * side),), device_id_type=MESH,
                )
                pl.when(there)(made.start)
                started.append((made, there))

    def finish():
        for made, there in started:
            pl.when(there)(made.wait_send)

    return [begin] + [functools.partial(step, t) for t in sum_order(p)] + [finish]


def scatter_body(length, many, extra, *refs):
    in_refs, extra_in, refs = refs[:many], refs[many : many + extra], refs[many + extra :]
    o_refs, extra_out, refs = refs[:many], refs[many : many + extra], refs[many + extra :]
    (pair_in, near, first_in, second_in, z_in, total,
     send_sem, pair_sem, load_sem, first_sem, second_sem, z_sem) = refs[:12]
    if extra:
        p, y, x, c, device = place(4)
        greet(4, p, device, y, x, c)
        work = line_sums(
            p, device, c, extra_in, extra_out, refs[12 : 12 + extra],
            refs[12 + extra : 12 + 2 * extra], *refs[12 + 2 * extra :]
        )
        p = p * 0
    else:
        p, y, x, c, device = place(length)
        greet(length, p, device, y, x, c)
        work = []
    half, width = total.shape
    order = sum_order(p) if length == 4 else [0]
    places = range(length)
    started = []

    def part(g, z, far, cc):
        if g % 2 == 0:
            return in_refs[g // 2].at[z, :, (1 - x if far else x), cc, 0]
        return in_refs[g // 2].at[z, (1 - y if far else y), :, cc, 1]

    def send(src, dst, slot, sem, target, there=None):
        made = pltpu.make_async_remote_copy(
            src_ref=src, dst_ref=dst, send_sem=send_sem.at[slot], recv_sem=sem,
            device_id=(target,), device_id_type=MESH,
        )
        if there is None:
            made.start()
        else:
            pl.when(there)(made.start)
        started.append((made, there))
        return made

    first_to = (device(x=1 - x), device(y=1 - y))
    second_to = (device(y=1 - y), device(x=1 - x))
    place_s = (y, x)
    slot = lambda g, z, k: (g * length + z) * 6 + k
    pairs, loads, firsts, seconds = {}, {}, {}, {}
    for begin in work[:2]:
        begin()
    steps = [(q, n) for q in range(many) for n in places]
    for q in range(many):
        for far in (1, 0):
            for n in places:
                z = order[n]
                for g in (2 * q, 2 * q + 1):
                    k = (g * length + z) * 2 + far
                    pairs[g, n, far] = send(
                        part(g, z, far, 1 - c), pair_in.at[g, z, far], slot(g, z, far),
                        pair_sem.at[k], device(c=1 - c),
                    )
                    loads[g, n, far] = pltpu.make_async_copy(
                        part(g, z, far, c), near.at[g, z, far], load_sem.at[k]
                    )
                    loads[g, n, far].start()

    def stage_first(q, n):
        z = order[n]
        for g in (2 * q, 2 * q + 1):
            pairs[g, n, 1].wait_recv()
            loads[g, n, 1].wait()
            for s in range(2):
                add_rows(near.at[g, z, 1, s], [near.at[g, z, 1, s], pair_in.at[g, z, 1, s]])
            firsts[g, n] = send(
                near.at[g, z, 1], first_in.at[g, z], slot(g, z, 2),
                first_sem.at[g * length + z], first_to[g % 2],
            )

    def stage_second(q, n):
        z = order[n]
        for g in (2 * q, 2 * q + 1):
            s = 1 - place_s[g % 2]
            pairs[g, n, 0].wait_recv()
            loads[g, n, 0].wait()
            firsts[g, n].wait_recv()
            add_rows(near.at[g, z, 0, s],
                [near.at[g, z, 0, s], pair_in.at[g, z, 0, s], first_in.at[g, z, s]])
            seconds[g, n] = send(
                near.at[g, z, 0, s], second_in.at[g, z], slot(g, z, 3),
                second_sem.at[g * length + z], second_to[g % 2],
            )

    def stage_z(q, n):
        z = order[n]
        for g in (2 * q, 2 * q + 1):
            s = place_s[g % 2]
            o_half = o_refs[q].at[g % 2]
            seconds[g, n].wait_recv()
            sources = [near.at[g, z, 0, s], pair_in.at[g, z, 0, s], first_in.at[g, z, s],
                       second_in.at[g, z]]
            if length == 1:
                add_rows(o_half, sources)
                continue
            add_rows(total, sources)
            for side, sender in ((0, (p > 0) & (p <= z)), (1, (p < length - 1) & (p >= z))):
                @pl.when(sender)
                def _():
                    k = (g * length + z) * 2 + side
                    pltpu.make_async_remote_copy(
                        src_ref=near.at[g, z, 0, s], dst_ref=z_in.at[g, z, side],
                        send_sem=send_sem.at[0], recv_sem=z_sem.at[k],
                        device_id=(device(c=1 - c),), device_id_type=MESH,
                    ).wait_recv()
                    add_rows(total, [total, z_in.at[g, z, side]])
            @pl.when(p == z)
            def _():
                add_rows(o_half, [total])
            @pl.when(p != z)
            def _():
                add_rows(near.at[g, z, 0, s], [total])
            send(near.at[g, z, 0, s], z_in.at[g, z, 0], slot(g, z, 4),
                 z_sem.at[(g * length + z) * 2], device(1), p < z)
            send(near.at[g, z, 0, s], z_in.at[g, z, 1], slot(g, z, 5),
                 z_sem.at[(g * length + z) * 2 + 1], device(-1), p > z)

    count = len(steps)
    for i in range(count + 3):
        for stage, j in ((stage_first, i), (stage_z, i - 3), (stage_second, i - 1)):
            if 0 <= j < count:
                stage(*steps[j])
                if stage is stage_first and work:
                    work[2]()
    for step in work[3:]:
        step()
    for made, there in started:
        if there is None:
            made.wait_send()
        else:
            pl.when(there)(made.wait_send)


def scatter(values, length, collective_id, others=()):
    many, extra = len(values), len(others)
    rows, width = values[0].shape[0] // (8 * length), values[0].shape[1]
    half = rows // 2
    kind = values[0].dtype
    lanes = 2 * many
    others = [other.reshape((4, other.shape[0] // 4) + other.shape[1:]) for other in others]
    extra_scratch = []
    if extra:
        extra_scratch = (
            [pltpu.VMEM(other.shape, other.dtype) for other in others]
            + [pltpu.VMEM((5,) + other.shape[1:], other.dtype) for other in others]
            + [pltpu.SemaphoreType.DMA((n * extra,)) for n in (4, 8, 8)]
        )
    outs = pl.pallas_call(
        functools.partial(scatter_body, length, many, extra),
        out_shape=[jax.ShapeDtypeStruct((2, half, width), FL)] * many
        + [jax.ShapeDtypeStruct(other.shape[1:], other.dtype) for other in others],
        in_specs=[pl.BlockSpec(memory_space=pl.ANY)] * (many + extra),
        out_specs=[pl.BlockSpec(memory_space=pltpu.VMEM)] * (many + extra),
        scratch_shapes=[
            pltpu.VMEM((lanes, length, 2, 2, half, width), kind),
            pltpu.VMEM((lanes, length, 2, 2, half, width), kind),
            pltpu.VMEM((lanes, length, 2, half, width), kind),
            pltpu.VMEM((lanes, length, half, width), kind),
            pltpu.VMEM((lanes, length, 2, half, width), kind),
            pltpu.VMEM((half, width), FL),
            pltpu.SemaphoreType.DMA((6 * lanes * length,)),
            pltpu.SemaphoreType.DMA((2 * lanes * length,)),
            pltpu.SemaphoreType.DMA((2 * lanes * length,)),
            pltpu.SemaphoreType.DMA((lanes * length,)),
            pltpu.SemaphoreType.DMA((lanes * length,)),
            pltpu.SemaphoreType.DMA((2 * lanes * length,)),
        ] + extra_scratch,
        compiler_params=pltpu.CompilerParams(
            collective_id=collective_id, has_side_effects=True, vmem_limit_bytes=62 << 20
        ),
    )(*[value.reshape(length, 2, 2, 2, 2, half, width) for value in values], *others)
    return [out.reshape(rows, width) for out in outs[:many]] + list(outs[many:])


def side_by_side(value, parts):
    blocks, rows, columns = value.shape
    columns = columns // parts

    def body(in_ref, out_ref):
        for part in range(parts):
            pieces = [
                in_ref[block].astype(FL)[:, part * columns : (part + 1) * columns]
                for block in range(blocks)
            ]
            lanes = pl.ds(part * blocks * columns, blocks * columns)
            out_ref[:, lanes] = jnp.concatenate(pieces, axis=1)

    return pl.pallas_call(
        body, out_shape=jax.ShapeDtypeStruct((rows, parts * blocks * columns), FL)
    )(value)


def dot(a, b, dims=((1,), (0,))):
    return lax.dot_general(a, b, (dims, ((), ())), preferred_element_type=FL)


def feed_body(mid_ref, grad_ref, weight_ref, w1_ref, w2_ref, part_ref, out_ref, act_ref, pre_ref,
              *, gate_column, shared_width):
    full = w2_ref.shape[0]
    mid, grad = mid_ref[...], grad_ref[...]
    pre = dot(mid, w1_ref[...])
    grad_act = dot(grad, w2_ref[...], ((1,), (1,)))
    gate_pre, up = pre[:, :full], pre[:, full:]
    shared_scale = jax.nn.sigmoid(gate_pre[:, gate_column : gate_column + 1])
    column = lax.broadcasted_iota(jnp.int32, gate_pre.shape, 1)
    factor = jnp.where(column < shared_width, shared_scale, weight_ref[...])
    sig = jax.nn.sigmoid(gate_pre)
    silu = gate_pre * sig
    act = silu * up
    low = (act * factor).astype(BF)
    logit = jnp.sum(
        act[:, :shared_width] * grad_act[:, :shared_width], axis=1, keepdims=True
    )
    d_logit = logit * shared_scale * (1.0 - shared_scale)
    scaled = grad_act * factor
    d_gate = scaled * up * sig * (1.0 + gate_pre * (1.0 - sig))
    d_gate = jnp.where(column == gate_column, d_logit, d_gate)
    act_ref[...] = low
    pre_ref[:, :full] = d_gate.astype(BF)
    pre_ref[:, full:] = (scaled * silu).astype(BF)
    part_ref[...] = dot(pre_ref[...], w1_ref[...], ((1,), (1,))).astype(BF)
    out_ref[...] = dot(low, w2_ref[...]).astype(BF)


def feed(mid, grad, weight, w1, w2, gate_column, shared_width):
    tokens, width = mid.shape
    full = w2.shape[0]
    block = 256
    row = lambda columns: pl.BlockSpec((block, columns), lambda i: (i, 0))
    whole = lambda shape: pl.BlockSpec(
        shape, lambda i: (0, 0), pipeline_mode=pl.Buffered(buffer_count=1)
    )
    return pl.pallas_call(
        functools.partial(feed_body, gate_column=gate_column, shared_width=shared_width),
        grid=(tokens // block,),
        out_shape=(
            jax.ShapeDtypeStruct((tokens, width), BF),
            jax.ShapeDtypeStruct((tokens, width), BF),
            jax.ShapeDtypeStruct((tokens, full), BF),
            jax.ShapeDtypeStruct((tokens, 2 * full), BF),
        ),
        in_specs=[row(width), row(width), row(1), whole(w1.shape), whole(w2.shape)],
        out_specs=(row(width), row(width), row(full), row(2 * full)),
        compiler_params=pltpu.CompilerParams(vmem_limit_bytes=56 << 20),
        cost_estimate=pl.CostEstimate(
            flops=12 * tokens * width * full, bytes_accessed=12 * tokens * width,
            transcendentals=tokens * full,
        ),
    )(mid, grad, weight, w1, w2)


def rms_norm(vector, factor):
    return vector * lax.rsqrt(jnp.mean(vector * vector, axis=-1, keepdims=True) + EPSILON) * factor


def rotate(vector, cosine, sine):
    middle = vector.shape[-1] // 2
    turned = jnp.concatenate([-vector[..., middle:], vector[..., :middle]], axis=-1)
    return vector * cosine + turned * sine


def unrotate(grad, cosine, sine):
    middle = grad.shape[-1] // 2
    scaled = grad * sine
    turned = jnp.concatenate([scaled[..., middle:], -scaled[..., :middle]], axis=-1)
    return grad * cosine + turned


def pair_weight_table(expert_ids, route_weights, order_row, expert_count, capacity):
    rows, top = expert_ids.shape
    pairs = rows * top
    flat = expert_ids.reshape(pairs)
    index = jnp.arange(pairs, dtype=jnp.int32)
    turn = jnp.sum(
        jnp.where(order_row[None, :] == index[:, None], index[None, :], 0), axis=1, dtype=jnp.int32
    )
    before = (turn[None, :] < turn[:, None]) & (flat[None, :] == flat[:, None])
    slots = jnp.sum(before.astype(jnp.int32), axis=1, dtype=jnp.int32)
    kept = (slots < capacity).astype(FL).reshape(rows, top)
    hit = expert_ids[:, :, None] == jnp.arange(expert_count, dtype=jnp.int32)[None, None, :]
    return jnp.sum(jnp.where(hit, (route_weights * kept)[:, :, None], 0.0), axis=1)


def per_device(
    tokens,
    cotangent,
    segment_ids,
    expert_ids,
    route_weights,
    pair_order,
    norm_in_gain,
    qkv_weight,
    qkv_bias,
    out_weight,
    norm_mid_gain,
    shared_gate,
    shared_in,
    shared_out,
    expert_in,
    expert_out,
):
    rows, width = tokens.shape
    count = lax.axis_size(AXIS)
    me = lax.axis_index(AXIS)
    team = SEQ // rows
    teams = count // team
    slab = me // team
    seat = me % team
    heads = width // HEAD_DIM
    own = heads // team
    span = own * HEAD_DIM
    top = expert_ids.shape[1]
    expert_count = count // EXP_PARTS
    capacity = (9 * rows * top + 8 * expert_count - 1) // (8 * expert_count)
    score_scale = HEAD_DIM ** (-0.5)
    in_team = [[s * team + p for p in range(team)] for s in range(teams)]
    across = [[s * team + p for s in range(teams)] for p in range(team)]
    share = width // count
    bias_share = 3 * width // count
    hid_s = shared_out.shape[0]
    hid_e = expert_out.shape[1]

    layered = team == 8 and teams == 4

    def team_gather(value, call):
        if layered:
            return gather(value, 1, call)
        return lax.all_gather(value, AXIS, axis=0, tiled=True, axis_index_groups=in_team)

    def team_scatter(value, call):
        if layered:
            return scatter([value], 1, call)[0]
        return lax.psum_scatter(
            value, AXIS, scatter_dimension=0, tiled=True, axis_index_groups=in_team
        )

    table = pair_weight_table(expert_ids, route_weights, pair_order[0], expert_count, capacity)
    packed = jnp.concatenate(
        [
            norm_in_gain.astype(FL),
            qkv_bias.astype(FL),
            norm_mid_gain.astype(FL),
            shared_gate.astype(FL),
            segment_ids.astype(FL),
            table.T.reshape(-1),
        ]
    )
    if layered:
        entries = packed.shape[0]
        lanes = -(-entries // 2048) * 128
        packed = jnp.pad(packed, (0, 16 * lanes - entries)).reshape(16, lanes)
        small = gather(packed, teams, 6).reshape(count, 16 * lanes)[:, :entries]
    else:
        small = lax.all_gather(packed[None], AXIS, axis=0, tiled=True)
    qkv_weight, small = lax.optimization_barrier((qkv_weight, small))
    edge = share
    gain_in = small[:, :edge].reshape(1, width)
    bias = small[:, edge : edge + bias_share].reshape(3, heads, HEAD_DIM)
    edge += bias_share
    gain_mid = small[:, edge : edge + share].reshape(1, width)
    edge += share
    gate = small[:, edge : edge + share].reshape(1, width)
    edge += share
    ids_all = small[:, edge : edge + rows]
    edge += rows
    tables = small[:, edge:].reshape(count, expert_count, rows)
    expert_weight = lax.dynamic_index_in_dim(tables, me // EXP_PARTS, 1, False).reshape(-1)

    mine = qkv_weight.reshape(share, 3, team, span).transpose(2, 0, 1, 3)
    mine = lax.all_to_all(
        mine.reshape(team, share, 3 * span),
        AXIS,
        split_axis=0,
        concat_axis=0,
        tiled=True,
        axis_index_groups=in_team,
    )
    deal = [(p * teams + s, s * team + p) for s in range(teams) for p in range(team)]
    mine = mine.reshape(team * share, 3 * span)
    out_rows = lax.ppermute(out_weight, AXIS, deal)
    inputs = tokens.astype(FL)
    scale_in = lax.rsqrt(jnp.mean(inputs * inputs, axis=-1, keepdims=True) + EPSILON)
    normed = (inputs * scale_in * gain_in).astype(BF)
    if layered:
        normed, w_qkv, w_out = layer_and_line(normed, [mine, out_rows], 0)
    else:
        normed = team_gather(normed, 0)
        w_qkv, w_out = [
            lax.all_gather(value, AXIS, axis=0, tiled=True, axis_index_groups=across)
            for value in (mine, out_rows)
        ]
    bias_own = lax.dynamic_slice_in_dim(bias, seat * own, own, 1).reshape(1, 3 * span)

    shared_in, normed = lax.optimization_barrier((shared_in, normed))

    shared_cols = shared_in.reshape(share, 2, count, hid_s).transpose(2, 0, 1, 3)
    w_shared = lax.all_to_all(
        shared_cols.reshape(count, share, 2 * hid_s),
        AXIS,
        split_axis=0,
        concat_axis=0,
        tiled=True,
    ).reshape(width, 2 * hid_s)
    grad_all = lax.all_gather(cotangent, AXIS, axis=0, tiled=True)

    own_ids = lax.dynamic_slice_in_dim(ids_all, slab * team, team, 0).reshape(SEQ)
    prev_ids = lax.dynamic_slice_in_dim(
        ids_all, jnp.maximum(slab - 1, 0) * team, team, 0
    ).reshape(SEQ)
    key_ids = jnp.concatenate([jnp.where(slab > 0, prev_ids, -1.0), own_ids])
    slot = jnp.arange(SEQ, dtype=jnp.int32)
    earlier = (key_ids[None, :] < own_ids[:, None]).astype(jnp.int32)
    positions = (SEQ + slot - jnp.sum(earlier, axis=1, dtype=jnp.int32)).astype(FL)
    inverse = THETA ** (-jnp.arange(0, HEAD_DIM, 2, dtype=FL) / HEAD_DIM)
    angles = positions[:, None] * inverse[None, :]
    angles = jnp.concatenate([angles, angles], axis=-1)
    cosine = jnp.cos(angles)[:, None, :]
    sine = jnp.sin(angles)[:, None, :]

    projected = dot(normed, w_qkv) + bias_own
    queries = rotate(projected[:, :span].reshape(SEQ, own, HEAD_DIM), cosine, sine).astype(BF)
    keys = rotate(projected[:, span : 2 * span].reshape(SEQ, own, HEAD_DIM), cosine, sine)
    key_value = jnp.stack([keys.astype(BF).reshape(SEQ, span), projected[:, 2 * span :].astype(BF)])
    forward = [(source, source + team) for source in range(count - team)]
    backward = [(target, source) for source, target in forward]
    passed = lax.ppermute(key_value, AXIS, forward)
    window = jnp.concatenate([passed, key_value], axis=1).reshape(2, 2 * SEQ, own, HEAD_DIM)
    allowed = (
        jnp.arange(2 * SEQ, dtype=jnp.int32)[None, :] <= slot[:, None] + SEQ
    ) & (key_ids[None, :] == own_ids[:, None])

    def masked_scores():
        scores = (
            jnp.einsum("qhd,khd->hqk", queries, window[0], preferred_element_type=FL) * score_scale
        )
        return jnp.where(allowed[None], scores, MASKED)

    scores = masked_scores()
    top_score = jnp.max(scores, axis=-1, keepdims=True)
    log_total = top_score + jnp.log(
        jnp.sum(jnp.exp(scores - top_score), axis=-1, keepdims=True)
    )
    probs = jnp.exp(scores - log_total).astype(BF)
    attended = jnp.einsum("hqk,khd->qhd", probs, window[1], preferred_element_type=FL)
    attended = attended.reshape(SEQ, span).astype(BF)
    hidden = inputs + team_scatter(dot(attended, w_out).astype(BF), 1).astype(FL)
    scale_mid = lax.rsqrt(jnp.mean(hidden * hidden, axis=-1, keepdims=True) + EPSILON)
    mid = (hidden * scale_mid * gain_mid).astype(BF)
    w_shared, mid = lax.optimization_barrier((w_shared, mid))
    wide_s = -(-(hid_s + 1) // 128) * 128
    wide_e = -(-hid_e // 128) * 128
    full = wide_s + wide_e

    def columns(value, wide):
        return jnp.pad(value, ((0, 0), (0, wide - value.shape[1])))

    gate_side = jnp.concatenate([w_shared[:, :hid_s], gate.reshape(width, 1).astype(BF)], axis=1)
    w1 = jnp.concatenate(
        [
            columns(gate_side, wide_s),
            columns(expert_in[0][:, :hid_e], wide_e),
            columns(w_shared[:, hid_s:], wide_s),
            columns(expert_in[0][:, hid_e:], wide_e),
        ],
        axis=1,
    )
    w2 = jnp.concatenate(
        [
            jnp.pad(shared_out, ((0, wide_s - hid_s), (0, 0))),
            jnp.pad(expert_out[0], ((0, wide_e - hid_e), (0, 0))),
        ],
        axis=0,
    )

    if layered:
        mid_all = gather(mid, teams, 2)
    else:
        mid_all = lax.all_gather(mid, AXIS, axis=0, tiled=True)
    mid_part, out_part, act_low, d_pre = feed(
        mid_all, grad_all, expert_weight[:, None], w1, w2, hid_s, wide_s
    )
    if layered:
        summed_mid, summed_out = scatter([mid_part, out_part], teams, 3)
    else:
        summed_mid = lax.psum_scatter(mid_part, AXIS, scatter_dimension=0, tiled=True)
        summed_out = lax.psum_scatter(out_part, AXIS, scatter_dimension=0, tiled=True)
    d_w1 = dot(mid_all, d_pre, ((0,), (0,)))
    d_w2 = dot(act_low, grad_all, ((0,), (0,)))
    expert_in_grad = jnp.concatenate(
        [d_w1[:, wide_s : wide_s + hid_e], d_w1[:, full + wide_s : full + wide_s + hid_e]], axis=1
    )
    d_shared = jnp.concatenate([d_w1[:, :hid_s], d_w1[:, full : full + hid_s]], axis=1)
    gate_grad = d_w1[:, hid_s]
    shared_back = lax.all_to_all(
        d_shared.astype(BF).reshape(count, share, 2 * hid_s),
        AXIS,
        split_axis=0,
        concat_axis=0,
        tiled=True,
    )
    output = (hidden + summed_out.astype(FL)).astype(BF)

    grad_out = cotangent.astype(FL)
    d_mid = summed_mid.astype(FL)

    def norm_back(value, scale, gain, grad):
        unit = value * scale
        weighted = grad * gain
        inner = jnp.mean(weighted * unit, axis=-1, keepdims=True)
        return scale * (weighted - unit * inner), jnp.sum(grad * unit, axis=0)

    d_hidden_part, gain_mid_grad = norm_back(hidden, scale_mid, gain_mid, d_mid)
    d_hidden = grad_out + d_hidden_part
    d_attn = team_gather(d_hidden.astype(BF), 4)
    d_attended = dot(d_attn, w_out, ((1,), (1,))).astype(BF)
    out_grad = dot(attended, d_attn, ((0,), (0,))).astype(BF)
    d_attended = d_attended.reshape(SEQ, own, HEAD_DIM)
    attention = jnp.exp(masked_scores() - log_total)
    d_attention = jnp.einsum("qhd,khd->hqk", d_attended, window[1], preferred_element_type=FL)
    row_delta = jnp.sum(attention * d_attention, axis=-1, keepdims=True)
    d_scores = (attention * (d_attention - row_delta)).astype(BF)
    d_queries = (
        jnp.einsum("hqk,khd->qhd", d_scores, window[0], preferred_element_type=FL) * score_scale
    )
    d_keys = jnp.einsum("hqk,qhd->khd", d_scores, queries, preferred_element_type=FL) * score_scale
    d_values = jnp.einsum(
        "hqk,qhd->khd", attention.astype(BF), d_attended, preferred_element_type=FL
    )
    d_kv = jnp.stack([d_keys.reshape(2 * SEQ, span), d_values.reshape(2 * SEQ, span)])
    returned = lax.ppermute(d_kv[:, :SEQ].astype(BF), AXIS, backward).astype(FL)
    d_kv = d_kv[:, SEQ:] + returned
    d_projected = jnp.concatenate(
        [
            unrotate(d_queries, cosine, sine).reshape(SEQ, span),
            unrotate(d_kv[0].reshape(SEQ, own, HEAD_DIM), cosine, sine).reshape(SEQ, span),
            d_kv[1],
        ],
        axis=1,
    ).astype(BF)
    d_projected, shared_back, d_w2 = lax.optimization_barrier((d_projected, shared_back, d_w2))
    d_normed = dot(d_projected, w_qkv, ((1,), (1,))).astype(BF)
    qkv_grad = dot(normed, d_projected, ((0,), (0,))).astype(BF)
    if layered:
        d_normed, qkv_part, out_part_grad = scatter([d_normed], 1, 5, [qkv_grad, out_grad])
    else:
        d_normed = team_scatter(d_normed, 5).astype(FL)
        qkv_part, out_part_grad = [
            lax.psum_scatter(
                value, AXIS, scatter_dimension=0, tiled=True, axis_index_groups=across
            )
            for value in (qkv_grad, out_grad)
        ]
    out_weight_grad = lax.ppermute(
        out_part_grad, AXIS, [(target, source) for source, target in deal]
    ).astype(FL)
    d_inputs, gain_in_grad = norm_back(inputs, scale_in, gain_in, d_normed)
    input_grad = d_hidden + d_inputs
    bias_grad = jnp.sum(d_projected.astype(FL), axis=0).reshape(3, own, HEAD_DIM)

    if layered:
        shared_in_grad = side_by_side(shared_back, 2)
    else:
        shared_in_grad = (
            shared_back.reshape(count, share, 2, hid_s)
            .transpose(1, 2, 0, 3)
            .reshape(share, -1)
            .astype(FL)
        )

    shared_out_grad = d_w2[:hid_s]
    expert_out_grad = d_w2[wide_s : wide_s + hid_e]
    qkv_part = lax.all_to_all(
        qkv_part.reshape(team, share, 3 * span),
        AXIS,
        split_axis=0,
        concat_axis=0,
        tiled=True,
        axis_index_groups=in_team,
    )
    qkv_weight_grad = (
        qkv_part.reshape(team, share, 3, span)
        .transpose(1, 2, 0, 3)
        .reshape(share, 3 * width)
        .astype(FL)
    )
    bias_spread = lax.dynamic_update_slice_in_dim(
        jnp.zeros((3, heads, HEAD_DIM), FL), bias_grad, seat * own, 1
    )
    small_grads = jnp.concatenate(
        [
            gain_in_grad.reshape(count, share),
            bias_spread.reshape(count, bias_share),
            gain_mid_grad.reshape(count, share),
            gate_grad.reshape(count, share),
        ],
        axis=1,
    )
    if layered:
        entries = small_grads.shape[1]
        lanes = -(-entries // 2048) * 128
        small_grads = jnp.pad(small_grads, ((0, 0), (0, 16 * lanes - entries)))
        small_sum = scatter([small_grads.reshape(count * 16, lanes)], teams, 7)[0]
        small_sum = small_sum.reshape(-1)[:entries]
    else:
        small_sum = lax.psum_scatter(small_grads, AXIS, scatter_dimension=0, tiled=True)[0]
    return (
        output,
        input_grad,
        small_sum[:share],
        qkv_weight_grad,
        small_sum[share : share + bias_share],
        out_weight_grad,
        small_sum[share + bias_share : 2 * share + bias_share],
        small_sum[2 * share + bias_share :],
        shared_in_grad,
        shared_out_grad,
        expert_in_grad[None],
        expert_out_grad[None],
    )


def solution(mesh):
    row, flat, deep = P("fsdp", None), P("fsdp"), P("fsdp", None, None)
    return jax.shard_map(
        per_device,
        mesh=mesh,
        in_specs=(
            row, row, flat, row, row, row, flat, row, flat, row, flat, flat, row, row, deep, deep,
        ),
        out_specs=(row, row, flat, row, flat, row, flat, flat, row, row, deep, deep),
        check_vma=False,
    )
```
